512 devices in a mesh: slab: 128 (over z, x, core), img: 4 (over y).
Axes of the slice: x: 4, y: 4, z: 16, core: 2. Of those that a mesh axis runs over, the one named last changes fastest.
Arguments:
- images: bfloat16 [65536, 2, 4, 512], P(('slab', 'img')), may hold values from -6 to 6
- pose_bins: int32 [65536], P(('slab', 'img')), may hold values from 0 to 8191, as said below
- labels: int32 [65536], P(('slab', 'img')), may hold values from 0 to 1
- defocus: bfloat16 [65536], P(('slab', 'img')), may hold values from 0.5 to 2
Outputs:
- maps: float32 [4, 1024, 2, 512], P('img', 'slab')
The draws below stay inside these ranges and needn't reach their ends.
Inputs may be any that keep to these rules, and one draw needn't show every extreme that they name: With owner = (pose_bins // 16) // 4: among the 128 images of one device (aligned blocks in order), no owner is named more than 2 times, and one owner, the same for all blocks, is named exactly 2 times in every block.
All inputs are finite; a program needn't handle non-finite values.
Results may differ from the reference program's by a relative error of at most 0.025.
Values may be sent and summed in bfloat16 or wider, within the bound.
A program may use at most 64 MiB of HBM per device.

```python
import math
import jax
import jax.numpy as jnp
from jax import lax

NX = 512
KY = 4
CLASSES = 2
ZDEV = 4
ZBINS = 4
XBINS = 4
IMG_DEV = 128
NZ = 512
IMAGES = 65536


def draw_pose_bins(key, part):
    owners = NZ // ZDEV
    capacity = 2 * IMG_DEV // owners
    slot_grand_count = owners * capacity
    level_key, hot_key, block_base = jax.random.split(key, 3)
    load_levels = jax.random.randint(level_key, (owners,), 0, 4)
    busiest_bins = jax.random.randint(hot_key, (), 0, owners)
    slot_holder_rank = jnp.arange(slot_grand_count, dtype=jnp.int32) // capacity

    def one_block(block_index):
        random_keys = jax.random.split(jax.random.fold_in(block_base, block_index), 6)
        popular_bin_holder = jax.random.randint(random_keys[0], (), 0, owners)
        random_jitter = jax.random.randint(random_keys[1], (slot_grand_count,), 0, 64)
        extra_score = jnp.where((slot_holder_rank == busiest_bins) | (slot_holder_rank == popular_bin_holder), 1000, 0)
        bin_score = (load_levels[slot_holder_rank] * 48 + random_jitter + extra_score) * slot_grand_count + jax.random.permutation(random_keys[2], slot_grand_count)
        ranked = lax.top_k(bin_score, IMG_DEV)[1]
        picked = ranked[jax.random.permutation(random_keys[3], IMG_DEV)]
        owner_of = picked // capacity
        planes = owner_of * ZDEV + jax.random.randint(random_keys[4], (IMG_DEV,), 0, ZDEV)
        remainder = jax.random.randint(random_keys[5], (IMG_DEV,), 0, ZBINS * XBINS)
        return (planes * (ZBINS * XBINS) + remainder).astype(jnp.int32)
    return jax.vmap(one_block)(jnp.arange(IMAGES // IMG_DEV, dtype=jnp.int32)).reshape(IMAGES)


def touch_ends(drawn, rng, smallest, largest):
    longest = drawn.shape.index(max(drawn.shape))
    spots = []
    for shift in (0, 1):
        where = [jax.random.randint(jax.random.fold_in(rng, axis), (), 0, length) for axis, length in enumerate(drawn.shape)]
        where[longest] = (where[longest] + shift) % drawn.shape[longest]
        spots.append(tuple(where))
    return drawn.at[spots[0]].set(smallest).at[spots[1]].set(largest)


def block_scale(rng, extent, cuts, least, top_value):
    def one(dim, parts):
        steps = jax.random.uniform(jax.random.fold_in(jax.random.fold_in(rng, 6), dim), (parts,), jnp.float32, least / len(cuts), top_value / len(cuts))
        return jnp.repeat(jnp.exp(steps), extent[dim] // parts).reshape((-1,) + (1,) * (len(extent) - dim - 1))

    level = one(*cuts[0])
    for cut in cuts[1:]:
        level = level * one(*cut)
    return level


def gaussian(own_key, extent, width, limit, cuts=(), kind=jnp.bfloat16):
    level = block_scale(own_key, extent, cuts, -0.22, 0.18) if cuts else 1.0
    values = jax.random.normal(own_key, extent, jnp.float32) * width * level
    return jnp.minimum(jnp.maximum(values, -limit), limit).astype(kind)


def setup_inputs(seed: int = 0) -> dict:
    streams_of = jax.random.split(jax.random.key(seed), 5)
    images = gaussian(streams_of[0], (IMAGES, 2, KY, NX), 1.0, 6.0, ((0, 512),))
    pose_bins = draw_pose_bins(jax.random.fold_in(streams_of[4], 71), 0)
    labels = touch_ends(jax.random.randint(streams_of[2], (IMAGES,), 0, CLASSES), jax.random.fold_in(streams_of[2], 1), 0, CLASSES - 1).astype(jnp.int32)
    defocus = jnp.clip(jnp.exp(math.log(2.0) - 1.3862944 * jax.random.uniform(streams_of[3], (IMAGES,), jnp.float32) ** block_scale(streams_of[3], (IMAGES,), ((0, 512),), -0.2, 0.2)), 0.5, 2.0).astype(jnp.bfloat16)
    return dict(images=images, pose_bins=pose_bins, labels=labels, defocus=defocus)


def lanczos_taps(fraction):
    offsets = jnp.arange(8, dtype=jnp.float32) - 3.0
    distance = offsets[None, :] - fraction[:, None]
    kernel = jnp.sinc(distance) * jnp.sinc(distance / 4.0)
    return (kernel / lax.optimization_barrier(jnp.sum(kernel, axis=-1, keepdims=True))).astype(jnp.bfloat16)

def ctf_weights(defocus, ky_rows, x_width):
    x_index = jnp.arange(x_width, dtype=jnp.int32)
    signed = (x_index + x_width // 2) % x_width - x_width // 2
    y_index = jnp.arange(ky_rows, dtype=jnp.int32) + 1
    radius = (y_index[:, None] * y_index[:, None] + signed[None, :] * signed[None, :]).astype(jnp.float32)
    radius = radius / float(x_width * x_width)
    phase_arg = 400.0 * math.pi * defocus.astype(jnp.float32)[:, None, None] * radius[None]
    return jnp.sin(phase_arg + 0.1)

def settle(values):
    return lax.optimization_barrier(values.astype(jnp.bfloat16)).astype(jnp.float32)

def reference(images, pose_bins, labels, defocus):
    per_pose = ZBINS * XBINS
    block_size = math.gcd(IMAGES, 1024)
    num_blocks = IMAGES // block_size

    def add_block(volume, block_index):
        first_row = block_index * block_size
        rows_now = lax.dynamic_slice_in_dim(images, first_row, block_size, 0)
        pose_rows = lax.dynamic_slice_in_dim(pose_bins, first_row, block_size, 0)
        label_rows = lax.dynamic_slice_in_dim(labels, first_row, block_size, 0)
        focus_rows = lax.dynamic_slice_in_dim(defocus, first_row, block_size, 0)
        weighted = settle(ctf_weights(focus_rows, KY, NX)[:, None] * rows_now.astype(jnp.float32))
        x_taps = lax.optimization_barrier(lanczos_taps(((pose_rows % XBINS).astype(jnp.float32) + 0.5) / XBINS)).astype(jnp.float32)
        summed = jnp.zeros(weighted.shape, jnp.float32)
        for tap_no in range(8):
            summed = summed + x_taps[:, tap_no][:, None, None, None] * jnp.roll(weighted, tap_no - 3, axis=3)
        placed = settle(summed)
        begin_plane = pose_rows // per_pose
        zbin_frac = (pose_rows // XBINS % ZBINS).astype(jnp.float32)
        z_taps = lax.optimization_barrier(lanczos_taps((zbin_frac + 0.5) / ZBINS)).astype(jnp.float32)
        planes = (begin_plane[:, None] + jnp.arange(8, dtype=jnp.int32)[None, :]) % NZ
        dest_rows = (label_rows[:, None] * NZ + planes).reshape(-1)
        contrib = (z_taps[:, :, None] * placed.reshape(block_size, 1, -1)).reshape(block_size * 8, -1)
        return (volume.at[dest_rows].add(contrib), None)
    volume = jnp.zeros((CLASSES * NZ, 2 * KY * NX), jnp.float32)
    volume, _ = lax.scan(add_block, volume, jnp.arange(num_blocks, dtype=jnp.int32))
    volume = volume.reshape(CLASSES, NZ, 2, KY, NX)
    cplx_vol = volume[:, :, 0] + 1j * volume[:, :, 1]
    spatial = jnp.fft.ifft2(cplx_vol, axes=(1, 3)) * (NZ * NX)
    stacked = jnp.stack([jnp.real(spatial), jnp.imag(spatial)], axis=0)
    stacked = jnp.transpose(stacked, (3, 1, 4, 0, 2)).reshape(KY, CLASSES * NX, 2, NZ)
    return (stacked * (2.5 / math.sqrt(IMAGES * NX))).astype(jnp.float32)
```

```python
import math

import jax
import jax.numpy as jnp
import ml_dtypes
import numpy as np
from jax import lax
from jax.experimental import pallas as pl
from jax.experimental.pallas import tpu as pltpu
from jax.sharding import PartitionSpec as P

NX = 512
KY = 4
NZ = 512
CLASSES = 2
ZBINS = 4
XBINS = 4
TAPS = 8
IMG_DEV = 128
IMAGES = 65536

ZC = 16
Q = 8
NY = 4
J = NX * CLASSES // (ZC * Q)
K = NX // (Q * J)
PLANE = NY * Q

MESH = pl.DeviceIdType.MESH


def tap_values(bins):
    fraction = (np.arange(bins) + 0.5) / bins
    distance = np.arange(TAPS)[None, :] - 3.0 - fraction[:, None]
    kernel = np.sinc(distance) * np.sinc(distance / 4.0)
    kernel = kernel / kernel.sum(axis=-1, keepdims=True)
    return kernel.astype(np.float32).astype(ml_dtypes.bfloat16).astype(np.float64)


def column_order():
    q, r, k, j = np.meshgrid(
        np.arange(Q), np.arange(2), np.arange(K), np.arange(J), indexing="ij"
    )
    return (k * Q * J + q * J + j).reshape(-1), r.reshape(-1)


def x_table():
    column, part = column_order()
    angle = 2 * np.pi / NX * ((np.arange(NX)[:, None] * column[None, :]) % NX)
    return np.where(part[None, :] == 0, np.cos(angle), np.sin(angle)).astype(
        ml_dtypes.bfloat16
    )


def z_table():
    index = np.arange(NZ)
    angle = 2 * np.pi / NZ * ((index[:, None] * index[None, :]) % NZ)
    return np.concatenate([np.cos(angle), np.sin(angle)], 1).astype(ml_dtypes.bfloat16)


def tap_transform():
    column, _ = column_order()
    taps = tap_values(XBINS)
    shift = np.arange(TAPS) - 3
    wave = np.exp(2j * np.pi / NX * ((shift[:, None] * column[None, :]) % NX))
    spectrum = taps @ wave
    both = np.stack([spectrum.real, spectrum.imag])
    high = both.astype(np.float32).astype(ml_dtypes.bfloat16)
    low = (both - high.astype(np.float64)).astype(np.float32).astype(ml_dtypes.bfloat16)
    return np.concatenate([high, low], axis=1)


def radius_table():
    signed = (np.arange(NX) + NX // 2) % NX - NX // 2
    rows = np.arange(KY) + 1
    return (rows[:, None] ** 2 + signed[None, :] ** 2).astype(np.float32)


def sine_coefficients(terms):
    nodes = 0.25 + 0.25 * np.cos(np.pi * (np.arange(400) + 0.5) / 400)
    f = np.sqrt(nodes) * np.sqrt(0.5)
    basis = f[:, None] ** (2 * np.arange(terms)[None, :] + 1)
    scale = np.abs(basis).max(0)
    fit = np.linalg.lstsq(basis / scale, np.sin(2 * np.pi * f), rcond=None)[0]
    return [float(v) for v in fit / scale]


SINE = sine_coefficients(8)


def sine_turns(turns):
    f = turns - jnp.round(turns)
    t = f * f
    value = jnp.full_like(t, SINE[-1])
    for c in SINE[-2::-1]:
        value = value * t + c
    return value * f


def insertion_kernel(
    focus_ref,
    images_ref,
    key_ref,
    radius_ref,
    xtab_ref,
    xtap_ref,
    ztab_ref,
    out_ref,
    rows_ref,
    factor_ref,
    send_ref,
    recv_ref,
    keys_ref,
    spread_ref,
    total_ref,
    zsend_ref,
    zrecv_ref,
    send_sem,
    recv_sem,
    ksend_sem,
    krecv_sem,
    zsend_sem,
    zrecv_sem,
):
    slab = lax.axis_index("slab")
    me_y = lax.axis_index("img")
    me_z = slab // Q
    me_q = lax.rem(slab, Q)

    def plane_peer(dy, dq):
        return me_z * Q + lax.rem(me_q + dq, Q), lax.rem(me_y + dy, NY)

    def z_peer(dz):
        return lax.rem(me_z + dz, ZC) * Q + me_q, me_y

    barrier = pltpu.get_barrier_semaphore()

    @pl.loop(1, PLANE)
    def _(step):
        pl.semaphore_signal(
            barrier,
            inc=1,
            device_id=plane_peer(step // Q, lax.rem(step, Q)),
            device_id_type=MESH,
        )

    @pl.loop(1, ZC)
    def _(step):
        pl.semaphore_signal(
            barrier, inc=1, device_id=z_peer(step), device_id_type=MESH
        )

    radius = radius_ref[...]

    @pl.loop(0, IMG_DEV, unroll=4)
    def _(i):
        ctf = sine_turns(focus_ref[i] * radius + 0.1 / (2 * math.pi))
        value = jnp.concatenate(
            [ctf * images_ref[i, r].astype(jnp.float32) for r in range(2)], axis=0
        )
        for b in range(NX // 128):
            rows_ref[b, pl.ds(pl.multiple_of(i * 8, 8), 8), :] = value[
                :, b * 128 : (b + 1) * 128
            ]

    key = key_ref[...]
    xbin = jnp.broadcast_to(key & (XBINS - 1), (8, IMG_DEV))
    row = lax.broadcasted_iota(jnp.int32, (8, IMG_DEV), 0)
    chosen = jnp.where(xbin == (row & (XBINS - 1)), 1.0, 0.0).astype(jnp.float32)
    chosen = jnp.concatenate(
        [chosen, jnp.zeros((IMG_DEV - 8, IMG_DEV), jnp.float32)], axis=0
    ).T[:, :8]
    chosen = chosen.astype(jnp.bfloat16)
    for part in range(2):
        factor_ref[part] = jnp.dot(
            chosen, xtap_ref[part], preferred_element_type=jnp.float32
        )

    pl.semaphore_wait(barrier, PLANE - 1 + ZC - 1)

    own_key = pltpu.make_async_copy(key_ref, keys_ref.at[0], krecv_sem)
    own_key.start()

    @pl.loop(1, PLANE)
    def _(step):
        pltpu.make_async_remote_copy(
            src_ref=key_ref,
            dst_ref=keys_ref.at[step],
            send_sem=ksend_sem,
            recv_sem=krecv_sem,
            device_id=plane_peer(step // Q, lax.rem(step, Q)),
            device_id_type=MESH,
        ).start()

    half = NX // K

    def transform(ky):
        both = jnp.concatenate(
            [
                jnp.concatenate(
                    [
                        rows_ref[b, pl.ds(r * KY + ky, IMG_DEV, stride=8), :]
                        for b in range(NX // 128)
                    ],
                    axis=1,
                )
                for r in range(2)
            ],
            axis=0,
        ).astype(jnp.bfloat16)
        product = jnp.dot(both, xtab_ref[...], preferred_element_type=jnp.float32)
        lane = lax.broadcasted_iota(jnp.int32, (IMG_DEV, 128), 1)
        sign = jnp.where(lane < half, -1.0, 1.0).astype(jnp.float32)
        for q in range(Q):
            lanes = slice(q * 128, (q + 1) * 128)
            real, imag = product[:IMG_DEV, lanes], product[IMG_DEV:, lanes]
            turned = sign * pltpu.roll(imag, half, 1)
            turned_real = sign * pltpu.roll(real, half, 1)
            value = factor_ref[0, :, lanes] * (real + turned) + factor_ref[
                1, :, lanes
            ] * (turned_real - imag)
            send_ref[ky * Q + q] = value.astype(jnp.bfloat16)

    def send_row(dy):
        ky = lax.rem(me_y + dy, NY)
        if dy == 0:
            pltpu.make_async_copy(
                send_ref.at[ky * Q + me_q], recv_ref.at[0], recv_sem.at[0]
            ).start()

        @pl.loop(1 if dy == 0 else 0, Q)
        def _(dq):
            pltpu.make_async_remote_copy(
                src_ref=send_ref.at[ky * Q + lax.rem(me_q + dq, Q)],
                dst_ref=recv_ref.at[dy * Q + dq],
                send_sem=send_sem,
                recv_sem=recv_sem.at[dy],
                device_id=plane_peer(dy, dq),
                device_id_type=MESH,
            ).start()

    order = (2, 1, 3, 0)
    for dy in order:
        transform(lax.rem(me_y + dy, NY))
        send_row(dy)

    pltpu.make_async_copy(keys_ref, keys_ref, krecv_sem).wait()
    ztaps = tap_values(ZBINS)
    sub = lax.broadcasted_iota(jnp.int32, (16, IMG_DEV), 0)

    @pl.loop(0, PLANE)
    def _(slot):
        entry = keys_ref[slot]
        zbin = (entry >> 2) & (ZBINS - 1)
        start = (entry >> 4) & (NZ - 1)
        label = entry >> 13
        low = jnp.broadcast_to(start & 15, (16, IMG_DEV))
        offset = (sub - low) & 15
        base = jnp.broadcast_to(start >> 4, (16, IMG_DEV))
        base = (base + jnp.where(sub < low, 1, 0)) & 31
        block = base + jnp.broadcast_to(label * 32, (16, IMG_DEV))
        pattern = jnp.zeros((16, IMG_DEV), jnp.float32)
        for t in range(TAPS):
            tap = jnp.full((1, IMG_DEV), float(ztaps[0, t]), jnp.float32)
            for b in range(1, ZBINS):
                tap = jnp.where(zbin == b, float(ztaps[b, t]), tap)
            pattern = jnp.where(
                offset == t, jnp.broadcast_to(tap, (16, IMG_DEV)), pattern
            )
        lanes = pl.ds(pl.multiple_of(lax.rem(slot, Q) * IMG_DEV, IMG_DEV), IMG_DEV)
        for b in range(CLASSES * NZ // 16):
            spread_ref[slot // Q, b * 16 : (b + 1) * 16, lanes] = jnp.where(
                block == b, pattern, 0.0
            ).astype(jnp.bfloat16)

    for n, dy in enumerate(order):
        arrived = recv_ref.at[pl.ds(dy * Q, Q)]
        pltpu.make_async_copy(arrived, arrived, recv_sem.at[dy]).wait()
        part = jnp.dot(
            spread_ref[dy],
            recv_ref[dy * Q : (dy + 1) * Q].reshape(Q * IMG_DEV, 128),
            preferred_element_type=jnp.float32,
        )
        total_ref[...] = part if n == 0 else total_ref[...] + part

    volume = total_ref[...].T
    for c in range(CLASSES):
        planes = slice(c * NZ, (c + 1) * NZ)
        for k in range(K):
            zsend_ref[c * K + k] = jnp.concatenate(
                [
                    volume[r * half + k * J : r * half + (k + 1) * J, planes]
                    for r in range(2)
                ],
                axis=0,
            ).astype(jnp.bfloat16)

    pltpu.make_async_copy(zsend_ref.at[me_z], zrecv_ref.at[0], zrecv_sem).start()

    @pl.loop(1, ZC)
    def _(dz):
        pltpu.make_async_remote_copy(
            src_ref=zsend_ref.at[lax.rem(me_z + dz, ZC)],
            dst_ref=zrecv_ref.at[dz],
            send_sem=zsend_sem,
            recv_sem=zrecv_sem,
            device_id=z_peer(dz),
            device_id_type=MESH,
        ).start()

    pltpu.make_async_copy(zrecv_ref, zrecv_ref, zrecv_sem).wait()

    columns = jnp.zeros((2 * J, NZ), jnp.float32)
    for dz in range(ZC):
        columns = columns + zrecv_ref[dz].astype(jnp.float32)
    high = columns.astype(jnp.bfloat16)
    low = (columns - high.astype(jnp.float32)).astype(jnp.bfloat16)
    waves = jnp.dot(
        jnp.concatenate([high, low], axis=0),
        ztab_ref[...],
        preferred_element_type=jnp.float32,
    )
    waves = (waves[: 2 * J] + waves[2 * J :]) * (2.5 / math.sqrt(IMAGES * NX))
    out_ref[0] = waves[:J, :NZ] - waves[J:, NZ:]
    out_ref[1] = waves[:J, NZ:] + waves[J:, :NZ]

    plane_sent = send_ref.at[pl.ds(0, PLANE - 1)]
    pltpu.make_async_copy(plane_sent, plane_sent, send_sem).wait()
    keys_sent = keys_ref.at[pl.ds(0, PLANE - 1)]
    pltpu.make_async_copy(keys_sent, keys_sent, ksend_sem).wait()
    z_sent = zsend_ref.at[pl.ds(0, ZC - 1)]
    pltpu.make_async_copy(z_sent, z_sent, zsend_sem).wait()


def on_device(images, pose_bins, labels, defocus):
    key = (labels * (NZ * ZBINS * XBINS) + pose_bins).reshape(1, IMG_DEV)
    focus = defocus.astype(jnp.float32) * (200.0 / (NX * NX))
    vmem = pl.BlockSpec(memory_space=pltpu.VMEM)
    out = pl.pallas_call(
        insertion_kernel,
        out_shape=jax.ShapeDtypeStruct((2, J, NZ), jnp.float32),
        in_specs=[pl.BlockSpec(memory_space=pltpu.SMEM)] + [vmem] * 6,
        out_specs=vmem,
        scratch_shapes=[
            pltpu.VMEM((NX // 128, IMG_DEV * 8, 128), jnp.float32),
            pltpu.VMEM((2, IMG_DEV, 2 * NX), jnp.float32),
            pltpu.VMEM((PLANE, IMG_DEV, 128), jnp.bfloat16),
            pltpu.VMEM((PLANE, IMG_DEV, 128), jnp.bfloat16),
            pltpu.VMEM((PLANE, 1, IMG_DEV), jnp.int32),
            pltpu.VMEM((NY, CLASSES * NZ, Q * IMG_DEV), jnp.bfloat16),
            pltpu.VMEM((CLASSES * NZ, 128), jnp.float32),
            pltpu.VMEM((ZC, 2 * J, NZ), jnp.bfloat16),
            pltpu.VMEM((ZC, 2 * J, NZ), jnp.bfloat16),
            pltpu.SemaphoreType.DMA,
            pltpu.SemaphoreType.DMA((NY,)),
            pltpu.SemaphoreType.DMA,
            pltpu.SemaphoreType.DMA,
            pltpu.SemaphoreType.DMA,
            pltpu.SemaphoreType.DMA,
        ],
        compiler_params=pltpu.CompilerParams(
            collective_id=0, has_side_effects=True, vmem_limit_bytes=48 * 1024 * 1024
        ),
    )(
        focus,
        images,
        key,
        jnp.asarray(radius_table()),
        jnp.asarray(x_table()),
        jnp.asarray(tap_transform()),
        jnp.asarray(z_table()),
    )
    return out.transpose(1, 0, 2)[None]


def solution(mesh):
    placed = (
        P(("slab", "img"), None, None, None),
        P(("slab", "img")),
        P(("slab", "img")),
        P(("slab", "img")),
    )
    return jax.shard_map(
        on_device,
        mesh=mesh,
        in_specs=placed,
        out_specs=P("img", "slab", None, None),
        check_vma=False,
    )
```

```python
import math

import jax
import jax.numpy as jnp
import ml_dtypes
import numpy as np
from jax import lax
from jax.experimental import pallas as pl
from jax.experimental.pallas import tpu as pltpu
from jax.sharding import PartitionSpec as P

NX = 512
KY = 4
NZ = 512
CLASSES = 2
ZBINS = 4
XBINS = 4
TAPS = 8
IMG_DEV = 128
IMAGES = 65536

ZC = 16
Q = 8
NY = 4
J = NX * CLASSES // (ZC * Q)
K = NX // (Q * J)
PLANE = NY * Q
LOADS = 4

MESH = pl.DeviceIdType.MESH


def tap_values(bins):
    fraction = (np.arange(bins) + 0.5) / bins
    distance = np.arange(TAPS)[None, :] - 3.0 - fraction[:, None]
    kernel = np.sinc(distance) * np.sinc(distance / 4.0)
    kernel = kernel / kernel.sum(axis=-1, keepdims=True)
    return kernel.astype(np.float32).astype(ml_dtypes.bfloat16).astype(np.float64)


def column_order():
    q, r, k, j = np.meshgrid(
        np.arange(Q), np.arange(2), np.arange(K), np.arange(J), indexing="ij"
    )
    return (k * Q * J + q * J + j).reshape(-1), r.reshape(-1)


def x_table():
    column, part = column_order()
    angle = 2 * np.pi / NX * ((np.arange(NX)[:, None] * column[None, :]) % NX)
    return np.where(part[None, :] == 0, np.cos(angle), np.sin(angle)).astype(
        ml_dtypes.bfloat16
    )


def z_table():
    index = np.arange(NZ)
    angle = 2 * np.pi / NZ * ((index[:, None] * index[None, :]) % NZ)
    return np.concatenate([np.cos(angle), np.sin(angle)], 1).astype(ml_dtypes.bfloat16)


def tap_transform():
    column, _ = column_order()
    taps = tap_values(XBINS)
    shift = np.arange(TAPS) - 3
    wave = np.exp(2j * np.pi / NX * ((shift[:, None] * column[None, :]) % NX))
    spectrum = taps @ wave
    both = np.stack([spectrum.real, spectrum.imag])
    high = both.astype(np.float32).astype(ml_dtypes.bfloat16)
    low = (both - high.astype(np.float64)).astype(np.float32).astype(ml_dtypes.bfloat16)
    return np.concatenate([high, low], axis=1)


def sine_coefficients(terms):
    nodes = 0.25 + 0.25 * np.cos(np.pi * (np.arange(400) + 0.5) / 400)
    f = np.sqrt(nodes) * np.sqrt(0.5)
    basis = f[:, None] ** (2 * np.arange(terms)[None, :] + 1)
    scale = np.abs(basis).max(0)
    fit = np.linalg.lstsq(basis / scale, np.sin(2 * np.pi * f), rcond=None)[0]
    return [float(v) for v in fit / scale]


SINE = sine_coefficients(8)


def sine_turns(turns):
    f = turns - jnp.round(turns)
    t = f * f
    value = jnp.full_like(t, SINE[-1])
    for c in SINE[-2::-1]:
        value = value * t + c
    return value * f


def insertion_kernel(
    focus_ref,
    key_ref,
    images_hbm,
    xtab_hbm,
    xtap_hbm,
    ztab_hbm,
    out_ref,
    images_ref,
    xtab_ref,
    xtap_ref,
    ztab_ref,
    rows_ref,
    factor_ref,
    send_ref,
    recv_ref,
    keys_ref,
    spread_ref,
    total_ref,
    zsend_ref,
    zrecv_ref,
    send_sem,
    recv_sem,
    ksend_sem,
    krecv_sem,
    zsend_sem,
    zrecv_sem,
    image_sem,
    table_sem,
):
    slab = lax.axis_index("slab")
    me_y = lax.axis_index("img")
    me_z = slab // Q
    me_q = lax.rem(slab, Q)

    def plane_peer(dy, dq):
        return me_z * Q + lax.rem(me_q + dq, Q), lax.rem(me_y + dy, NY)

    def z_peer(dz):
        return lax.rem(me_z + dz, ZC) * Q + me_q, me_y

    barrier = pltpu.get_barrier_semaphore()

    @pl.loop(1, PLANE)
    def _(step):
        pl.semaphore_signal(
            barrier,
            inc=1,
            device_id=plane_peer(step // Q, lax.rem(step, Q)),
            device_id_type=MESH,
        )

    @pl.loop(1, ZC)
    def _(step):
        pl.semaphore_signal(
            barrier, inc=1, device_id=z_peer(step), device_id_type=MESH
        )

    per = IMG_DEV // LOADS
    loads = [
        pltpu.make_async_copy(
            images_hbm.at[pl.ds(n * per, per)],
            images_ref.at[pl.ds(n * per, per)],
            image_sem.at[n],
        )
        for n in range(LOADS)
    ]
    tables = [
        pltpu.make_async_copy(source, target, table_sem.at[n])
        for n, (source, target) in enumerate(
            [(xtap_hbm, xtap_ref), (xtab_hbm, xtab_ref), (ztab_hbm, ztab_ref)]
        )
    ]
    for copy in loads + tables:
        copy.start()

    x = lax.broadcasted_iota(jnp.int32, (KY, NX), 1)
    signed = ((x + NX // 2) & (NX - 1)) - NX // 2
    y = lax.broadcasted_iota(jnp.int32, (KY, NX), 0) + 1
    radius = (y * y + signed * signed).astype(jnp.float32)

    def weigh(i):
        ctf = sine_turns(focus_ref[i] * radius + 0.1 / (2 * math.pi))
        value = jnp.concatenate(
            [ctf * images_ref[i, r].astype(jnp.float32) for r in range(2)], axis=0
        )
        for b in range(NX // 128):
            rows_ref[b, pl.ds(pl.multiple_of(i * 8, 8), 8), :] = value[
                :, b * 128 : (b + 1) * 128
            ]

    for n in range(LOADS):
        loads[n].wait()
        pl.loop(n * per, (n + 1) * per, unroll=4)(weigh)

    tables[0].wait()
    key = key_ref[...]
    xbin = jnp.broadcast_to(key & (XBINS - 1), (8, IMG_DEV))
    row = lax.broadcasted_iota(jnp.int32, (8, IMG_DEV), 0)
    chosen = jnp.where(xbin == (row & (XBINS - 1)), 1.0, 0.0).astype(jnp.float32)
    chosen = jnp.concatenate(
        [chosen, jnp.zeros((IMG_DEV - 8, IMG_DEV), jnp.float32)], axis=0
    ).T[:, :8]
    chosen = chosen.astype(jnp.bfloat16)
    for part in range(2):
        factor_ref[part] = jnp.dot(
            chosen, xtap_ref[part], preferred_element_type=jnp.float32
        )

    tables[1].wait()

    half = NX // K

    def transform(ky):
        both = jnp.concatenate(
            [
                jnp.concatenate(
                    [
                        rows_ref[b, pl.ds(r * KY + ky, IMG_DEV, stride=8), :]
                        for b in range(NX // 128)
                    ],
                    axis=1,
                )
                for r in range(2)
            ],
            axis=0,
        ).astype(jnp.bfloat16)
        product = jnp.dot(both, xtab_ref[...], preferred_element_type=jnp.float32)
        lane = lax.broadcasted_iota(jnp.int32, (IMG_DEV, 128), 1)
        sign = jnp.where(lane < half, -1.0, 1.0).astype(jnp.float32)
        for q in range(Q):
            lanes = slice(q * 128, (q + 1) * 128)
            real, imag = product[:IMG_DEV, lanes], product[IMG_DEV:, lanes]
            turned = sign * pltpu.roll(imag, half, 1)
            turned_real = sign * pltpu.roll(real, half, 1)
            value = factor_ref[0, :, lanes] * (real + turned) + factor_ref[
                1, :, lanes
            ] * (turned_real - imag)
            send_ref[ky * Q + q] = value.astype(jnp.bfloat16)

    def send_row(dy):
        ky = lax.rem(me_y + dy, NY)
        if dy == 0:
            pltpu.make_async_copy(
                send_ref.at[ky * Q + me_q], recv_ref.at[0], recv_sem.at[0]
            ).start()

        @pl.loop(1 if dy == 0 else 0, Q)
        def _(dq):
            pltpu.make_async_remote_copy(
                src_ref=send_ref.at[ky * Q + lax.rem(me_q + dq, Q)],
                dst_ref=recv_ref.at[dy * Q + dq],
                send_sem=send_sem,
                recv_sem=recv_sem.at[dy],
                device_id=plane_peer(dy, dq),
                device_id_type=MESH,
            ).start()

    order = (2, 1, 3, 0)
    for n, dy in enumerate(order):
        transform(lax.rem(me_y + dy, NY))
        if n == 0:
            pl.semaphore_wait(barrier, PLANE - 1 + ZC - 1)
            pltpu.make_async_copy(key_ref, keys_ref.at[0], krecv_sem).start()

            @pl.loop(1, PLANE)
            def _(step):
                pltpu.make_async_remote_copy(
                    src_ref=key_ref,
                    dst_ref=keys_ref.at[step],
                    send_sem=ksend_sem,
                    recv_sem=krecv_sem,
                    device_id=plane_peer(step // Q, lax.rem(step, Q)),
                    device_id_type=MESH,
                ).start()

        send_row(dy)

    pltpu.make_async_copy(keys_ref, keys_ref, krecv_sem).wait()
    ztaps = tap_values(ZBINS)
    sub = lax.broadcasted_iota(jnp.int32, (16, IMG_DEV), 0)

    @pl.loop(0, PLANE)
    def _(slot):
        entry = keys_ref[slot]
        zbin = (entry >> 2) & (ZBINS - 1)
        start = (entry >> 4) & (NZ - 1)
        label = entry >> 13
        low = jnp.broadcast_to(start & 15, (16, IMG_DEV))
        offset = (sub - low) & 15
        base = jnp.broadcast_to(start >> 4, (16, IMG_DEV))
        base = (base + jnp.where(sub < low, 1, 0)) & 31
        block = base + jnp.broadcast_to(label * 32, (16, IMG_DEV))
        pattern = jnp.zeros((16, IMG_DEV), jnp.float32)
        for t in range(TAPS):
            tap = jnp.full((1, IMG_DEV), float(ztaps[0, t]), jnp.float32)
            for b in range(1, ZBINS):
                tap = jnp.where(zbin == b, float(ztaps[b, t]), tap)
            pattern = jnp.where(
                offset == t, jnp.broadcast_to(tap, (16, IMG_DEV)), pattern
            )
        lanes = pl.ds(pl.multiple_of(lax.rem(slot, Q) * IMG_DEV, IMG_DEV), IMG_DEV)
        for b in range(CLASSES * NZ // 16):
            spread_ref[slot // Q, b * 16 : (b + 1) * 16, lanes] = jnp.where(
                block == b, pattern, 0.0
            ).astype(jnp.bfloat16)

    for n, dy in enumerate(order):
        arrived = recv_ref.at[pl.ds(dy * Q, Q)]
        pltpu.make_async_copy(arrived, arrived, recv_sem.at[dy]).wait()
        part = jnp.dot(
            spread_ref[dy],
            recv_ref[dy * Q : (dy + 1) * Q].reshape(Q * IMG_DEV, 128),
            preferred_element_type=jnp.float32,
        )
        total_ref[...] = part if n == 0 else total_ref[...] + part

    volume = total_ref[...].T
    for c in range(CLASSES):
        planes = slice(c * NZ, (c + 1) * NZ)
        for k in range(K):
            zsend_ref[c * K + k] = jnp.concatenate(
                [
                    volume[r * half + k * J : r * half + (k + 1) * J, planes]
                    for r in range(2)
                ],
                axis=0,
            ).astype(jnp.bfloat16)

    pltpu.make_async_copy(zsend_ref.at[me_z], zrecv_ref.at[0], zrecv_sem).start()

    far_first = [ZC // 2]
    for d in range(ZC // 2 - 1, 0, -1):
        far_first += [d, ZC - d]
    for dz in far_first:
        pltpu.make_async_remote_copy(
            src_ref=zsend_ref.at[lax.rem(me_z + dz, ZC)],
            dst_ref=zrecv_ref.at[dz],
            send_sem=zsend_sem,
            recv_sem=zrecv_sem,
            device_id=z_peer(dz),
            device_id_type=MESH,
        ).start()

    tables[2].wait()
    pltpu.make_async_copy(zrecv_ref, zrecv_ref, zrecv_sem).wait()

    columns = jnp.zeros((2 * J, NZ), jnp.float32)
    for dz in range(ZC):
        columns = columns + zrecv_ref[dz].astype(jnp.float32)
    high = columns.astype(jnp.bfloat16)
    low = (columns - high.astype(jnp.float32)).astype(jnp.bfloat16)
    waves = jnp.dot(
        jnp.concatenate([high, low], axis=0),
        ztab_ref[...],
        preferred_element_type=jnp.float32,
    )
    waves = (waves[: 2 * J] + waves[2 * J :]) * (2.5 / math.sqrt(IMAGES * NX))
    out_ref[0] = waves[:J, :NZ] - waves[J:, NZ:]
    out_ref[1] = waves[:J, NZ:] + waves[J:, :NZ]

    plane_sent = send_ref.at[pl.ds(0, PLANE - 1)]
    pltpu.make_async_copy(plane_sent, plane_sent, send_sem).wait()
    keys_sent = keys_ref.at[pl.ds(0, PLANE - 1)]
    pltpu.make_async_copy(keys_sent, keys_sent, ksend_sem).wait()
    z_sent = zsend_ref.at[pl.ds(0, ZC - 1)]
    pltpu.make_async_copy(z_sent, z_sent, zsend_sem).wait()


def on_device(images, pose_bins, labels, defocus):
    key = (labels * (NZ * ZBINS * XBINS) + pose_bins).reshape(1, IMG_DEV)
    focus = defocus.astype(jnp.float32) * (200.0 / (NX * NX))
    vmem = pl.BlockSpec(memory_space=pltpu.VMEM)
    out = pl.pallas_call(
        insertion_kernel,
        out_shape=jax.ShapeDtypeStruct((2, J, NZ), jnp.float32),
        in_specs=[pl.BlockSpec(memory_space=pltpu.SMEM), vmem]
        + [pl.BlockSpec(memory_space=pl.ANY)] * 4,
        out_specs=vmem,
        scratch_shapes=[
            pltpu.VMEM(images.shape, jnp.bfloat16),
            pltpu.VMEM((NX, 2 * NX), jnp.bfloat16),
            pltpu.VMEM((2, 8, 2 * NX), jnp.bfloat16),
            pltpu.VMEM((NZ, 2 * NZ), jnp.bfloat16),
            pltpu.VMEM((NX // 128, IMG_DEV * 8, 128), jnp.float32),
            pltpu.VMEM((2, IMG_DEV, 2 * NX), jnp.float32),
            pltpu.VMEM((PLANE, IMG_DEV, 128), jnp.bfloat16),
            pltpu.VMEM((PLANE, IMG_DEV, 128), jnp.bfloat16),
            pltpu.VMEM((PLANE, 1, IMG_DEV), jnp.int32),
            pltpu.VMEM((NY, CLASSES * NZ, Q * IMG_DEV), jnp.bfloat16),
            pltpu.VMEM((CLASSES * NZ, 128), jnp.float32),
            pltpu.VMEM((ZC, 2 * J, NZ), jnp.bfloat16),
            pltpu.VMEM((ZC, 2 * J, NZ), jnp.bfloat16),
            pltpu.SemaphoreType.DMA,
            pltpu.SemaphoreType.DMA((NY,)),
            pltpu.SemaphoreType.DMA,
            pltpu.SemaphoreType.DMA,
            pltpu.SemaphoreType.DMA,
            pltpu.SemaphoreType.DMA,
            pltpu.SemaphoreType.DMA((LOADS,)),
            pltpu.SemaphoreType.DMA((3,)),
        ],
        compiler_params=pltpu.CompilerParams(
            collective_id=0, has_side_effects=True, vmem_limit_bytes=60 * 1024 * 1024
        ),
    )(
        focus,
        key,
        images,
        jnp.asarray(x_table()),
        jnp.asarray(tap_transform()),
        jnp.asarray(z_table()),
    )
    return out.transpose(1, 0, 2)[None]


def solution(mesh):
    placed = (
        P(("slab", "img"), None, None, None),
        P(("slab", "img")),
        P(("slab", "img")),
        P(("slab", "img")),
    )
    return jax.shard_map(
        on_device,
        mesh=mesh,
        in_specs=placed,
        out_specs=P("img", "slab", None, None),
        check_vma=False,
    )
```

```python
import math

import jax
import jax.numpy as jnp
import ml_dtypes
import numpy as np
from jax import lax
from jax.experimental import pallas as pl
from jax.experimental.pallas import tpu as pltpu
from jax.sharding import PartitionSpec as P

NX = 512
KY = 4
NZ = 512
CLASSES = 2
ZBINS = 4
XBINS = 4
TAPS = 8
IMG_DEV = 128
IMAGES = 65536

ZC = 16
Q = 8
NY = 4
J = NX * CLASSES // (ZC * Q)
K = NX // (Q * J)
PLANE = NY * Q
LOADS = 4
CHUNKS = 2
KC = K // CHUNKS
ROWS = KC * J

MESH = pl.DeviceIdType.MESH
BIG = pltpu.HBM


def tap_values(bins):
    fraction = (np.arange(bins) + 0.5) / bins
    distance = np.arange(TAPS)[None, :] - 3.0 - fraction[:, None]
    kernel = np.sinc(distance) * np.sinc(distance / 4.0)
    kernel = kernel / kernel.sum(axis=-1, keepdims=True)
    return kernel.astype(np.float32).astype(ml_dtypes.bfloat16).astype(np.float64)


def chunk_columns():
    n, q, k, j = np.meshgrid(
        np.arange(CHUNKS), np.arange(Q), np.arange(KC), np.arange(J), indexing="ij"
    )
    return (CHUNKS * k + n) * Q * J + q * J + j


def x_table():
    column = chunk_columns().reshape(CHUNKS, Q, 1, KC * J, 1)
    angle = 2 * np.pi / NX * ((column * np.arange(NX)) % NX)
    both = np.concatenate([np.cos(angle), np.sin(angle)], axis=2)
    return both.reshape(CHUNKS, Q * 2 * KC * J, NX).astype(ml_dtypes.bfloat16)


def z_table():
    index = np.arange(NZ)
    angle = 2 * np.pi / NZ * ((index[:, None] * index[None, :]) % NZ)
    return np.concatenate([np.cos(angle), np.sin(angle)], 1).astype(ml_dtypes.bfloat16)


def tap_transform():
    column = chunk_columns().reshape(-1)
    shift = np.arange(TAPS) - 3
    wave = np.exp(2j * np.pi / NX * ((column[:, None] * shift[None, :]) % NX))
    spectrum = wave @ tap_values(XBINS).T
    both = np.stack([spectrum.real, spectrum.imag])
    high = both.astype(np.float32).astype(ml_dtypes.bfloat16)
    low = (both - high.astype(np.float64)).astype(np.float32).astype(ml_dtypes.bfloat16)
    return np.concatenate([high, low], axis=2)


def sine_coefficients(terms):
    nodes = 0.25 + 0.25 * np.cos(np.pi * (np.arange(400) + 0.5) / 400)
    f = np.sqrt(nodes) * np.sqrt(0.5)
    basis = f[:, None] ** (2 * np.arange(terms)[None, :] + 1)
    scale = np.abs(basis).max(0)
    fit = np.linalg.lstsq(basis / scale, np.sin(2 * np.pi * f), rcond=None)[0]
    return [float(v) for v in fit / scale]


SINE = sine_coefficients(8)


def sine_turns(turns):
    f = turns - jnp.round(turns)
    t = f * f
    value = jnp.full_like(t, SINE[-1])
    for c in SINE[-2::-1]:
        value = value * t + c
    return value * f


def nt_dot(a, b):
    return lax.dot_general(
        a, b, (((1,), (1,)), ((), ())), preferred_element_type=jnp.float32
    )


def insertion_kernel(
    pose_ref,
    label_ref,
    focus_ref,
    images_hbm,
    xtab_hbm,
    xtap_hbm,
    ztab_hbm,
    out_ref,
    images_ref,
    xtab_ref,
    xtap_ref,
    ztab_ref,
    depth_ref,
    rows_ref,
    both_ref,
    factor_ref,
    send_ref,
    recv_ref,
    key_ref,
    keys_ref,
    spread_ref,
    zsend_ref,
    zrecv_ref,
    send_sem,
    recv_sem,
    ksend_sem,
    krecv_sem,
    zsend_sem,
    zrecv_sem,
    image_sem,
    table_sem,
):
    slab = lax.axis_index("slab")
    me_y = lax.axis_index("img")
    me_z = slab // Q
    me_q = lax.rem(slab, Q)

    def plane_peer(dy, dq):
        return me_z * Q + lax.rem(me_q + dq, Q), lax.rem(me_y + dy, NY)

    def z_peer(dz):
        return lax.rem(me_z + dz, ZC) * Q + me_q, me_y

    per = IMG_DEV // LOADS
    loads = [
        pltpu.make_async_copy(
            images_hbm.at[pl.ds(n * per, per)],
            images_ref.at[pl.ds(n * per, per)],
            image_sem.at[n],
        )
        for n in range(LOADS)
    ]
    tables = [
        pltpu.make_async_copy(source, target, table_sem.at[n])
        for n, (source, target) in enumerate(
            [(xtap_hbm, xtap_ref), (xtab_hbm, xtab_ref), (ztab_hbm, ztab_ref)]
        )
    ]
    for copy in loads + tables:
        copy.start()

    barrier = pltpu.get_barrier_semaphore()

    @pl.loop(1, ZC)
    def _(step):
        pl.semaphore_signal(
            barrier, inc=1, device_id=z_peer(step), device_id_type=MESH
        )

    @pl.loop(1, PLANE)
    def _(step):
        pl.semaphore_signal(
            barrier,
            inc=1,
            device_id=plane_peer(step // Q, lax.rem(step, Q)),
            device_id_type=MESH,
        )

    key = label_ref[...] * (NZ * ZBINS * XBINS) + pose_ref[...]
    key_ref[...] = key
    depth_ref[...] = jnp.broadcast_to(
        focus_ref[...].astype(jnp.float32) * (200.0 / (NX * NX)), (IMG_DEV, IMG_DEV)
    ).T
    x = lax.broadcasted_iota(jnp.int32, (KY, NX), 1)
    signed = ((x + NX // 2) & (NX - 1)) - NX // 2
    y = lax.broadcasted_iota(jnp.int32, (KY, NX), 0) + 1
    radius = (y * y + signed * signed).astype(jnp.float32)

    def weigh(i):
        depth = jnp.broadcast_to(depth_ref[pl.ds(i, 1), :], (KY, 128))
        depth = jnp.concatenate([depth] * (NX // 128), axis=1)
        ctf = sine_turns(depth * radius + 0.1 / (2 * math.pi))
        value = jnp.concatenate(
            [ctf * images_ref[i, r].astype(jnp.float32) for r in range(2)], axis=0
        )
        for b in range(NX // 128):
            rows_ref[b, pl.ds(pl.multiple_of(i * 8, 8), 8), :] = value[
                :, b * 128 : (b + 1) * 128
            ]

    for n in range(LOADS):
        loads[n].wait()
        pl.loop(n * per, (n + 1) * per, unroll=4)(weigh)

    tables[0].wait()
    row = lax.broadcasted_iota(jnp.int32, (8, IMG_DEV), 0)
    xbin = jnp.broadcast_to(key & (XBINS - 1), (8, IMG_DEV))
    chosen = jnp.where(xbin == (row & (XBINS - 1)), 1.0, 0.0).astype(jnp.bfloat16)
    for part in range(2):
        factor_ref[part] = jnp.dot(
            xtap_ref[part], chosen, preferred_element_type=jnp.float32
        )
    tables[1].wait()

    def gather(ky):
        for r in range(2):
            for b in range(NX // 128):
                both_ref[
                    ky, r * IMG_DEV : (r + 1) * IMG_DEV, b * 128 : (b + 1) * 128
                ] = rows_ref[b, pl.ds(r * KY + ky, IMG_DEV, stride=8), :].astype(
                    jnp.bfloat16
                )

    def transform(chunk, ky):
        product = nt_dot(xtab_ref[chunk], both_ref[ky])
        for q in range(Q):
            top = q * 2 * ROWS
            cosine = product[top : top + ROWS]
            sine = product[top + ROWS : top + 2 * ROWS]
            real = cosine[:, :IMG_DEV] - sine[:, IMG_DEV:]
            imag = sine[:, :IMG_DEV] + cosine[:, IMG_DEV:]
            at = slice((chunk * Q + q) * ROWS, (chunk * Q + q + 1) * ROWS)
            tap_real, tap_imag = factor_ref[0, at], factor_ref[1, at]
            send_ref[chunk, ky * Q + q] = jnp.concatenate(
                [
                    real * tap_real - imag * tap_imag,
                    real * tap_imag + imag * tap_real,
                ],
                axis=0,
            ).astype(jnp.bfloat16)

    def send_row(chunk, dy):
        ky = lax.rem(me_y + dy, NY)
        if dy == 0:
            pltpu.make_async_copy(
                send_ref.at[chunk, ky * Q + me_q],
                recv_ref.at[chunk, 0],
                recv_sem.at[chunk, 0],
            ).start()

        @pl.loop(1 if dy == 0 else 0, Q)
        def _(dq):
            pltpu.make_async_remote_copy(
                src_ref=send_ref.at[chunk, ky * Q + lax.rem(me_q + dq, Q)],
                dst_ref=recv_ref.at[chunk, dy * Q + dq],
                send_sem=send_sem.at[chunk],
                recv_sem=recv_sem.at[chunk, dy],
                device_id=plane_peer(dy, dq),
                device_id_type=MESH,
            ).start()

    order = (2, 1, 3, 0)
    for chunk in range(CHUNKS):
        for n, dy in enumerate(order):
            ky = lax.rem(me_y + dy, NY)
            if chunk == 0:
                gather(ky)
            transform(chunk, ky)
            if chunk == 0 and n == 0:
                pl.semaphore_wait(barrier, PLANE - 1 + ZC - 1)
                pltpu.make_async_copy(key_ref, keys_ref.at[0], krecv_sem).start()

                @pl.loop(1, PLANE)
                def _(step):
                    pltpu.make_async_remote_copy(
                        src_ref=key_ref,
                        dst_ref=keys_ref.at[step],
                        send_sem=ksend_sem,
                        recv_sem=krecv_sem,
                        device_id=plane_peer(step // Q, lax.rem(step, Q)),
                        device_id_type=MESH,
                    ).start()

            send_row(chunk, dy)

    pltpu.make_async_copy(keys_ref, keys_ref, krecv_sem).wait()
    ztaps = tap_values(ZBINS)
    sub = lax.broadcasted_iota(jnp.int32, (16, IMG_DEV), 0)

    @pl.loop(0, PLANE)
    def _(slot):
        entry = keys_ref[slot]
        zbin = (entry >> 2) & (ZBINS - 1)
        start = (entry >> 4) & (NZ - 1)
        label = entry >> 13
        low = jnp.broadcast_to(start & 15, (16, IMG_DEV))
        offset = (sub - low) & 15
        base = jnp.broadcast_to(start >> 4, (16, IMG_DEV))
        base = (base + jnp.where(sub < low, 1, 0)) & 31
        block = base + jnp.broadcast_to(label * 32, (16, IMG_DEV))
        pattern = jnp.zeros((16, IMG_DEV), jnp.float32)
        for t in range(TAPS):
            tap = jnp.full((1, IMG_DEV), float(ztaps[0, t]), jnp.float32)
            for b in range(1, ZBINS):
                tap = jnp.where(zbin == b, float(ztaps[b, t]), tap)
            pattern = jnp.where(
                offset == t, jnp.broadcast_to(tap, (16, IMG_DEV)), pattern
            )
        lanes = pl.ds(pl.multiple_of(lax.rem(slot, Q) * IMG_DEV, IMG_DEV), IMG_DEV)
        for b in range(CLASSES * NZ // 16):
            spread_ref[slot // Q, b * 16 : (b + 1) * 16, lanes] = jnp.where(
                block == b, pattern, 0.0
            ).astype(jnp.bfloat16)

    odd = lax.rem(me_z, 2)
    for chunk in range(CHUNKS):
        volume = None
        for dy in order:
            arrived = recv_ref.at[chunk, pl.ds(dy * Q, Q)]
            pltpu.make_async_copy(arrived, arrived, recv_sem.at[chunk, dy]).wait()
            part = nt_dot(
                jnp.concatenate(
                    [recv_ref[chunk, dy * Q + q] for q in range(Q)], axis=1
                ),
                spread_ref[dy],
            )
            volume = part if volume is None else volume + part
        for c in range(CLASSES):
            planes = slice(c * NZ, (c + 1) * NZ)
            for k in range(KC):
                zsend_ref[c * K + k * CHUNKS + chunk] = jnp.concatenate(
                    [
                        volume[r * ROWS + k * J : r * ROWS + (k + 1) * J, planes]
                        for r in range(2)
                    ],
                    axis=0,
                ).astype(jnp.bfloat16)

        apart = lax.rem(odd + chunk, 2)

        def to_z(dz):
            pltpu.make_async_remote_copy(
                src_ref=zsend_ref.at[lax.rem(me_z + dz, ZC)],
                dst_ref=zrecv_ref.at[dz],
                send_sem=zsend_sem,
                recv_sem=zrecv_sem,
                device_id=z_peer(dz),
                device_id_type=MESH,
            ).start()

        same = [8, 6, 10, 4, 12, 2, 14]
        other = [7, 9, 5, 11, 3, 13, 1]
        for a, b in zip(same, other):
            to_z(a + apart * (b - a))

        @pl.when(apart == 1)
        def _():
            to_z(ZC - 1)

        @pl.when(apart == 0)
        def _():
            pltpu.make_async_copy(
                zsend_ref.at[me_z], zrecv_ref.at[0], zrecv_sem
            ).start()

    tables[2].wait()
    pltpu.make_async_copy(zrecv_ref, zrecv_ref, zrecv_sem).wait()

    columns = jnp.zeros((2 * J, NZ), jnp.float32)
    for dz in range(ZC):
        columns = columns + zrecv_ref[dz].astype(jnp.float32)
    high = columns.astype(jnp.bfloat16)
    low = (columns - high.astype(jnp.float32)).astype(jnp.bfloat16)
    waves = jnp.dot(
        jnp.concatenate([high, low], axis=0),
        ztab_ref[...],
        preferred_element_type=jnp.float32,
    )
    waves = (waves[: 2 * J] + waves[2 * J :]) * (2.5 / math.sqrt(IMAGES * NX))
    out_ref[0] = waves[:J, :NZ] - waves[J:, NZ:]
    out_ref[1] = waves[:J, NZ:] + waves[J:, :NZ]

    for chunk in range(CHUNKS):
        plane_sent = send_ref.at[chunk, pl.ds(0, PLANE - 1)]
        pltpu.make_async_copy(plane_sent, plane_sent, send_sem.at[chunk]).wait()
    keys_sent = keys_ref.at[pl.ds(0, PLANE - 1)]
    pltpu.make_async_copy(keys_sent, keys_sent, ksend_sem).wait()
    z_sent = zsend_ref.at[pl.ds(0, ZC - 1)]
    pltpu.make_async_copy(z_sent, z_sent, zsend_sem).wait()


def on_device(images, pose_bins, labels, defocus):
    vmem = pl.BlockSpec(memory_space=pltpu.VMEM)
    out = pl.pallas_call(
        insertion_kernel,
        out_shape=jax.ShapeDtypeStruct((2, J, NZ), jnp.float32),
        in_specs=[vmem] * 3 + [pl.BlockSpec(memory_space=BIG)] * 4,
        out_specs=vmem,
        scratch_shapes=[
            pltpu.VMEM(images.shape, jnp.bfloat16),
            pltpu.VMEM((CHUNKS, NX, NX), jnp.bfloat16),
            pltpu.VMEM((2, NX, 8), jnp.bfloat16),
            pltpu.VMEM((NZ, 2 * NZ), jnp.bfloat16),
            pltpu.VMEM((IMG_DEV, IMG_DEV), jnp.float32),
            pltpu.VMEM((NX // 128, IMG_DEV * 8, 128), jnp.float32),
            pltpu.VMEM((KY, 2 * IMG_DEV, NX), jnp.bfloat16),
            pltpu.VMEM((2, NX, IMG_DEV), jnp.float32),
            pltpu.VMEM((CHUNKS, PLANE, 2 * ROWS, IMG_DEV), jnp.bfloat16),
            pltpu.VMEM((CHUNKS, PLANE, 2 * ROWS, IMG_DEV), jnp.bfloat16),
            pltpu.VMEM((1, IMG_DEV), jnp.int32),
            pltpu.VMEM((PLANE, 1, IMG_DEV), jnp.int32),
            pltpu.VMEM((NY, CLASSES * NZ, Q * IMG_DEV), jnp.bfloat16),
            pltpu.VMEM((ZC, 2 * J, NZ), jnp.bfloat16),
            pltpu.VMEM((ZC, 2 * J, NZ), jnp.bfloat16),
            pltpu.SemaphoreType.DMA((CHUNKS,)),
            pltpu.SemaphoreType.DMA((CHUNKS, NY)),
            pltpu.SemaphoreType.DMA,
            pltpu.SemaphoreType.DMA,
            pltpu.SemaphoreType.DMA,
            pltpu.SemaphoreType.DMA,
            pltpu.SemaphoreType.DMA((LOADS,)),
            pltpu.SemaphoreType.DMA((3,)),
        ],
        compiler_params=pltpu.CompilerParams(
            collective_id=0, has_side_effects=True, vmem_limit_bytes=55040 * 1024
        ),
    )(
        pose_bins.reshape(1, IMG_DEV),
        labels.reshape(1, IMG_DEV),
        defocus.reshape(1, IMG_DEV),
        images,
        jnp.asarray(x_table()),
        jnp.asarray(tap_transform()),
        jnp.asarray(z_table()),
    )
    return out.transpose(1, 0, 2)[None]


def solution(mesh):
    placed = (
        P(("slab", "img"), None, None, None),
        P(("slab", "img")),
        P(("slab", "img")),
        P(("slab", "img")),
    )
    return jax.shard_map(
        on_device,
        mesh=mesh,
        in_specs=placed,
        out_specs=P("img", "slab", None, None),
        check_vma=False,
    )
```

```python
import math

import jax
import jax.numpy as jnp
import ml_dtypes
import numpy as np
from jax import lax
from jax.experimental import pallas as pl
from jax.experimental.pallas import tpu as pltpu
from jax.sharding import PartitionSpec as P

NX = 512
KY = 4
NZ = 512
CLASSES = 2
ZBINS = 4
XBINS = 4
TAPS = 8
IMG_DEV = 128
IMAGES = 65536

ZC = 16
Q = 8
NY = 4
J = NX * CLASSES // (ZC * Q)
K = NX // (Q * J)
PLANE = NY * Q
LOADS = 4
CHUNKS = 4
KC = K // CHUNKS
ROWS = KC * J
FAR_FIRST = sorted(range(1, ZC // CHUNKS), key=lambda n: abs(n * CHUNKS - ZC // 2))
ACROSS = [(dx, flip) for dx in (2, 1, 3, 0) for flip in (0, 1)]
ROW_GROUPS = ((2,), (1, 3), (0,))

MESH = pl.DeviceIdType.MESH
BIG = pltpu.HBM


def tap_values(bins):
    fraction = (np.arange(bins) + 0.5) / bins
    distance = np.arange(TAPS)[None, :] - 3.0 - fraction[:, None]
    kernel = np.sinc(distance) * np.sinc(distance / 4.0)
    kernel = kernel / kernel.sum(axis=-1, keepdims=True)
    return kernel.astype(np.float32).astype(ml_dtypes.bfloat16).astype(np.float64)


def chunk_columns():
    n, q, k, j = np.meshgrid(
        np.arange(CHUNKS), np.arange(Q), np.arange(KC), np.arange(J), indexing="ij"
    )
    return (CHUNKS * k + n) * Q * J + q * J + j


def x_table():
    column = chunk_columns().reshape(CHUNKS, Q, 1, KC * J, 1)
    angle = 2 * np.pi / NX * ((column * np.arange(NX)) % NX)
    both = np.concatenate([np.cos(angle), np.sin(angle)], axis=2)
    return both.reshape(CHUNKS, Q * 2 * KC * J, NX).astype(ml_dtypes.bfloat16)


def z_table():
    index = np.arange(NZ)
    angle = 2 * np.pi / NZ * ((index[:, None] * index[None, :]) % NZ)
    return np.concatenate([np.cos(angle), np.sin(angle)], 1).astype(ml_dtypes.bfloat16)


def tap_transform():
    column = chunk_columns().reshape(-1)
    shift = np.arange(TAPS) - 3
    wave = np.exp(2j * np.pi / NX * ((column[:, None] * shift[None, :]) % NX))
    spectrum = wave @ tap_values(XBINS).T
    both = np.stack([spectrum.real, spectrum.imag])
    high = both.astype(np.float32).astype(ml_dtypes.bfloat16)
    low = (both - high.astype(np.float64)).astype(np.float32).astype(ml_dtypes.bfloat16)
    return np.concatenate([high, low], axis=2)


def sine_coefficients(terms):
    nodes = 0.25 + 0.25 * np.cos(np.pi * (np.arange(400) + 0.5) / 400)
    f = np.sqrt(nodes) * np.sqrt(0.5)
    basis = f[:, None] ** (2 * np.arange(terms)[None, :] + 1)
    scale = np.abs(basis).max(0)
    fit = np.linalg.lstsq(basis / scale, np.sin(2 * np.pi * f), rcond=None)[0]
    return [float(v) for v in fit / scale]


SINE = sine_coefficients(7)


def sine_turns(turns):
    f = turns - jnp.round(turns)
    t = f * f
    value = jnp.full_like(t, SINE[-1])
    for c in SINE[-2::-1]:
        value = value * t + c
    return value * f


def nt_dot(a, b):
    return lax.dot_general(
        a, b, (((1,), (1,)), ((), ())), preferred_element_type=jnp.float32
    )


def insertion_kernel(
    pose_ref,
    label_ref,
    focus_ref,
    images_hbm,
    xtab_hbm,
    xtap_hbm,
    ztab_hbm,
    out_ref,
    images_ref,
    xtab_ref,
    xtap_ref,
    ztab_ref,
    depth_ref,
    rows_ref,
    both_ref,
    factor_ref,
    send_ref,
    recv_ref,
    key_ref,
    keys_ref,
    spread_ref,
    zsend_ref,
    zrecv_ref,
    send_sem,
    recv_sem,
    ksend_sem,
    krecv_sem,
    zsend_sem,
    zrecv_sem,
    image_sem,
    table_sem,
):
    slab = lax.axis_index("slab")
    me_y = lax.axis_index("img")
    me_z = slab // Q
    me_q = lax.rem(slab, Q)
    me_x, me_core = me_q // 2, lax.rem(me_q, 2)
    peer_q = {
        (dx, flip): lax.rem(me_x + dx, Q // 2) * 2 + lax.rem(me_core + flip, 2)
        for dx, flip in ACROSS
    }
    peer_y = [lax.rem(me_y + dy, NY) for dy in range(NY)]
    partners = [
        (dy, across)
        for group in ROW_GROUPS
        for across in ACROSS
        for dy in group
        if (dy, across) != (0, (0, 0))
    ]

    def plane_peer(dy, across):
        return me_z * Q + peer_q[across], peer_y[dy]

    def slot_of(dy, across):
        return dy * Q + across[0] * 2 + across[1]

    def z_peer(dz):
        return lax.rem(me_z + dz, ZC) * Q + me_q, me_y

    per = IMG_DEV // LOADS
    loads = [
        pltpu.make_async_copy(
            images_hbm.at[pl.ds(n * per, per)],
            images_ref.at[pl.ds(n * per, per)],
            image_sem.at[n],
        )
        for n in range(LOADS)
    ]
    tables = [
        pltpu.make_async_copy(source, target, table_sem.at[n])
        for n, (source, target) in enumerate(
            [(xtap_hbm, xtap_ref), (xtab_hbm, xtab_ref), (ztab_hbm, ztab_ref)]
        )
    ]
    for copy in loads + tables:
        copy.start()

    barrier = pltpu.get_barrier_semaphore()

    @pl.loop(1, ZC)
    def _(step):
        pl.semaphore_signal(
            barrier, inc=1, device_id=z_peer(step), device_id_type=MESH
        )

    for partner in partners:
        pl.semaphore_signal(
            barrier, inc=1, device_id=plane_peer(*partner), device_id_type=MESH
        )

    key = label_ref[...] * (NZ * ZBINS * XBINS) + pose_ref[...]
    key_ref[...] = key
    depth_ref[...] = jnp.broadcast_to(
        focus_ref[...].astype(jnp.float32) * (200.0 / (NX * NX)), (IMG_DEV, IMG_DEV)
    ).T

    def unpack(i):
        value = jnp.concatenate(
            [images_ref[i, r].astype(jnp.float32) for r in range(2)], axis=0
        )
        for b in range(NX // 128):
            rows_ref[b, pl.ds(pl.multiple_of(i * 8, 8), 8), :] = value[
                :, b * 128 : (b + 1) * 128
            ]

    for n in range(LOADS):
        loads[n].wait()
        pl.loop(n * per, (n + 1) * per, unroll=8)(unpack)

    tables[0].wait()
    row = lax.broadcasted_iota(jnp.int32, (8, IMG_DEV), 0)
    xbin = jnp.broadcast_to(key & (XBINS - 1), (8, IMG_DEV))
    chosen = jnp.where(xbin == (row & (XBINS - 1)), 1.0, 0.0).astype(jnp.bfloat16)
    for part in range(2):
        factor_ref[part] = jnp.dot(
            xtap_ref[part], chosen, preferred_element_type=jnp.float32
        )
    tables[1].wait()

    lane = lax.broadcasted_iota(jnp.int32, (1, 128), 1)

    def weigh(ky):
        for b in range(NX // 128):
            signed = (
                ((lane + (b * 128 + NX // 2)) & (NX - 1)) - NX // 2
            )
            radius = (signed * signed + (ky + 1) * (ky + 1)).astype(jnp.float32)
            ctf = sine_turns(depth_ref[...] * radius + 0.1 / (2 * math.pi))
            for r in range(2):
                image = rows_ref[b, pl.ds(r * KY + ky, IMG_DEV, stride=8), :]
                both_ref[
                    ky, r * IMG_DEV : (r + 1) * IMG_DEV, b * 128 : (b + 1) * 128
                ] = (ctf * image).astype(jnp.bfloat16)

    def transform(chunk, ky):
        product = nt_dot(xtab_ref[chunk], both_ref[ky])
        for q in range(Q):
            top = q * 2 * ROWS
            cosine = product[top : top + ROWS]
            sine = product[top + ROWS : top + 2 * ROWS]
            real = cosine[:, :IMG_DEV] - sine[:, IMG_DEV:]
            imag = sine[:, :IMG_DEV] + cosine[:, IMG_DEV:]
            at = slice((chunk * Q + q) * ROWS, (chunk * Q + q + 1) * ROWS)
            tap_real, tap_imag = factor_ref[0, at], factor_ref[1, at]
            send_ref[chunk, ky * Q + q] = jnp.concatenate(
                [
                    real * tap_real - imag * tap_imag,
                    real * tap_imag + imag * tap_real,
                ],
                axis=0,
            ).astype(jnp.bfloat16)

    def send(chunk, dy, across):
        slot = slot_of(dy, across)
        block = send_ref.at[chunk, peer_y[dy] * Q + peer_q[across]]
        if slot == 0:
            pltpu.make_async_copy(
                block, recv_ref.at[chunk, 0], recv_sem.at[chunk, 0]
            ).start()
        else:
            pltpu.make_async_remote_copy(
                src_ref=block,
                dst_ref=recv_ref.at[chunk, slot],
                send_sem=send_sem.at[chunk],
                recv_sem=recv_sem.at[chunk, dy],
                device_id=plane_peer(dy, across),
                device_id_type=MESH,
            ).start()

    def send_keys():
        pltpu.make_async_copy(key_ref, keys_ref.at[0], krecv_sem).start()
        for partner in partners:
            pltpu.make_async_remote_copy(
                src_ref=key_ref,
                dst_ref=keys_ref.at[slot_of(*partner)],
                send_sem=ksend_sem,
                recv_sem=krecv_sem,
                device_id=plane_peer(*partner),
                device_id_type=MESH,
            ).start()

    for chunk in range(CHUNKS):
        for group in ROW_GROUPS:
            for dy in group:
                if chunk == 0:
                    weigh(peer_y[dy])
                transform(chunk, peer_y[dy])
            if chunk == 0 and group == ROW_GROUPS[0]:
                pl.semaphore_wait(barrier, PLANE - 1 + ZC - 1)
                send_keys()
            for across in ACROSS:
                for dy in group:
                    send(chunk, dy, across)

    pltpu.make_async_copy(keys_ref, keys_ref, krecv_sem).wait()
    ztaps = tap_values(ZBINS)
    sub = lax.broadcasted_iota(jnp.int32, (16, IMG_DEV), 0)

    @pl.loop(0, PLANE)
    def _(slot):
        entry = keys_ref[slot]
        zbin = (entry >> 2) & (ZBINS - 1)
        start = (entry >> 4) & (NZ - 1)
        label = entry >> 13
        low = jnp.broadcast_to(start & 15, (16, IMG_DEV))
        offset = (sub - low) & 15
        base = jnp.broadcast_to(start >> 4, (16, IMG_DEV))
        base = (base + jnp.where(sub < low, 1, 0)) & 31
        block = base + jnp.broadcast_to(label * 32, (16, IMG_DEV))
        pattern = jnp.zeros((16, IMG_DEV), jnp.float32)
        for t in range(TAPS):
            tap = jnp.full((1, IMG_DEV), float(ztaps[0, t]), jnp.float32)
            for b in range(1, ZBINS):
                tap = jnp.where(zbin == b, float(ztaps[b, t]), tap)
            pattern = jnp.where(
                offset == t, jnp.broadcast_to(tap, (16, IMG_DEV)), pattern
            )
        lanes = pl.ds(pl.multiple_of(lax.rem(slot, Q) * IMG_DEV, IMG_DEV), IMG_DEV)
        for b in range(CLASSES * NZ // 16):
            spread_ref[slot // Q, b * 16 : (b + 1) * 16, lanes] = jnp.where(
                block == b, pattern, 0.0
            ).astype(jnp.bfloat16)

    for chunk in range(CHUNKS):
        volume = None
        for dy in (dy for group in ROW_GROUPS for dy in group):
            arrived = recv_ref.at[chunk, pl.ds(dy * Q, Q)]
            pltpu.make_async_copy(arrived, arrived, recv_sem.at[chunk, dy]).wait()
            part = nt_dot(
                jnp.concatenate(
                    [recv_ref[chunk, dy * Q + q] for q in range(Q)], axis=1
                ),
                spread_ref[dy],
            )
            volume = part if volume is None else volume + part
        for c in range(CLASSES):
            planes = slice(c * NZ, (c + 1) * NZ)
            for k in range(KC):
                zsend_ref[c * K + k * CHUNKS + chunk] = jnp.concatenate(
                    [
                        volume[r * ROWS + k * J : r * ROWS + (k + 1) * J, planes]
                        for r in range(2)
                    ],
                    axis=0,
                ).astype(jnp.bfloat16)

        apart = lax.rem(me_z * (CHUNKS - 1) + chunk, CHUNKS)

        def to_z(dz):
            pltpu.make_async_remote_copy(
                src_ref=zsend_ref.at[lax.rem(me_z + dz, ZC)],
                dst_ref=zrecv_ref.at[dz],
                send_sem=zsend_sem,
                recv_sem=zrecv_sem,
                device_id=z_peer(dz),
                device_id_type=MESH,
            ).start()

        for far in FAR_FIRST:
            to_z(apart + far * CHUNKS)

        @pl.when(apart != 0)
        def _():
            to_z(apart)

        @pl.when(apart == 0)
        def _():
            pltpu.make_async_copy(
                zsend_ref.at[me_z], zrecv_ref.at[0], zrecv_sem
            ).start()

    tables[2].wait()
    pltpu.make_async_copy(zrecv_ref, zrecv_ref, zrecv_sem).wait()

    columns = jnp.zeros((2 * J, NZ), jnp.float32)
    for dz in range(ZC):
        columns = columns + zrecv_ref[dz].astype(jnp.float32)
    high = columns.astype(jnp.bfloat16)
    low = (columns - high.astype(jnp.float32)).astype(jnp.bfloat16)
    waves = jnp.dot(
        jnp.concatenate([high, low], axis=0),
        ztab_ref[...],
        preferred_element_type=jnp.float32,
    )
    waves = (waves[: 2 * J] + waves[2 * J :]) * (2.5 / math.sqrt(IMAGES * NX))
    out_ref[0] = waves[:J, :NZ] - waves[J:, NZ:]
    out_ref[1] = waves[:J, NZ:] + waves[J:, :NZ]

    for chunk in range(CHUNKS):
        plane_sent = send_ref.at[chunk, pl.ds(0, PLANE - 1)]
        pltpu.make_async_copy(plane_sent, plane_sent, send_sem.at[chunk]).wait()
    keys_sent = keys_ref.at[pl.ds(0, PLANE - 1)]
    pltpu.make_async_copy(keys_sent, keys_sent, ksend_sem).wait()
    z_sent = zsend_ref.at[pl.ds(0, ZC - 1)]
    pltpu.make_async_copy(z_sent, z_sent, zsend_sem).wait()


def on_device(images, pose_bins, labels, defocus):
    vmem = pl.BlockSpec(memory_space=pltpu.VMEM)
    out = pl.pallas_call(
        insertion_kernel,
        out_shape=jax.ShapeDtypeStruct((2, J, NZ), jnp.float32),
        in_specs=[vmem] * 3 + [pl.BlockSpec(memory_space=BIG)] * 4,
        out_specs=vmem,
        scratch_shapes=[
            pltpu.VMEM(images.shape, jnp.bfloat16),
            pltpu.VMEM((CHUNKS, 2 * NX // CHUNKS, NX), jnp.bfloat16),
            pltpu.VMEM((2, NX, 8), jnp.bfloat16),
            pltpu.VMEM((NZ, 2 * NZ), jnp.bfloat16),
            pltpu.VMEM((IMG_DEV, IMG_DEV), jnp.float32),
            pltpu.VMEM((NX // 128, IMG_DEV * 8, 128), jnp.float32),
            pltpu.VMEM((KY, 2 * IMG_DEV, NX), jnp.bfloat16),
            pltpu.VMEM((2, NX, IMG_DEV), jnp.float32),
            pltpu.VMEM((CHUNKS, PLANE, 2 * ROWS, IMG_DEV), jnp.bfloat16),
            pltpu.VMEM((CHUNKS, PLANE, 2 * ROWS, IMG_DEV), jnp.bfloat16),
            pltpu.VMEM((1, IMG_DEV), jnp.int32),
            pltpu.VMEM((PLANE, 1, IMG_DEV), jnp.int32),
            pltpu.VMEM((NY, CLASSES * NZ, Q * IMG_DEV), jnp.bfloat16),
            pltpu.VMEM((ZC, 2 * J, NZ), jnp.bfloat16),
            pltpu.VMEM((ZC, 2 * J, NZ), jnp.bfloat16),
            pltpu.SemaphoreType.DMA((CHUNKS,)),
            pltpu.SemaphoreType.DMA((CHUNKS, NY)),
            pltpu.SemaphoreType.DMA,
            pltpu.SemaphoreType.DMA,
            pltpu.SemaphoreType.DMA,
            pltpu.SemaphoreType.DMA,
            pltpu.SemaphoreType.DMA((LOADS,)),
            pltpu.SemaphoreType.DMA((3,)),
        ],
        compiler_params=pltpu.CompilerParams(
            collective_id=0, has_side_effects=True, vmem_limit_bytes=55040 * 1024
        ),
    )(
        pose_bins.reshape(1, IMG_DEV),
        labels.reshape(1, IMG_DEV),
        defocus.reshape(1, IMG_DEV),
        images,
        jnp.asarray(x_table()),
        jnp.asarray(tap_transform()),
        jnp.asarray(z_table()),
    )
    return out.transpose(1, 0, 2)[None]


def solution(mesh):
    placed = (
        P(("slab", "img"), None, None, None),
        P(("slab", "img")),
        P(("slab", "img")),
        P(("slab", "img")),
    )
    return jax.shard_map(
        on_device,
        mesh=mesh,
        in_specs=placed,
        out_specs=P("img", "slab", None, None),
        check_vma=False,
    )
```

```python
import math

import jax
import jax.numpy as jnp
import ml_dtypes
import numpy as np
from jax import lax
from jax.experimental import pallas as pl
from jax.experimental.pallas import tpu as pltpu
from jax.sharding import PartitionSpec as P

NX = 512
KY = 4
NZ = 512
CLASSES = 2
ZBINS = 4
XBINS = 4
TAPS = 8
IMG_DEV = 128
IMAGES = 65536

ZC = 16
Q = 8
NY = 4
J = NX * CLASSES // (ZC * Q)
K = NX // (Q * J)
PLANE = NY * Q
LOADS = 4
CHUNKS = 4
KC = K // CHUNKS
ROWS = KC * J
TOGETHER = ((0,), (1,), (2,), (3,))
ACROSS = [(dx, flip) for dx in (2, 1, 3, 0) for flip in (0, 1)]
ROW_GROUPS = ((2,), (1, 3), (0,))

MESH = pl.DeviceIdType.MESH
BIG = pltpu.HBM


def tap_values(bins):
    fraction = (np.arange(bins) + 0.5) / bins
    distance = np.arange(TAPS)[None, :] - 3.0 - fraction[:, None]
    kernel = np.sinc(distance) * np.sinc(distance / 4.0)
    kernel = kernel / kernel.sum(axis=-1, keepdims=True)
    return kernel.astype(np.float32).astype(ml_dtypes.bfloat16).astype(np.float64)


def chunk_columns():
    n, q, k, j = np.meshgrid(
        np.arange(CHUNKS), np.arange(Q), np.arange(KC), np.arange(J), indexing="ij"
    )
    return (KC * n + k) * Q * J + q * J + j


def x_table():
    column = chunk_columns().reshape(CHUNKS, Q, 1, KC * J, 1)
    angle = 2 * np.pi / NX * ((column * np.arange(NX)) % NX)
    both = np.concatenate([np.cos(angle), np.sin(angle)], axis=2)
    return both.reshape(CHUNKS, Q * 2 * KC * J, NX).astype(ml_dtypes.bfloat16)


def z_table():
    index = np.arange(NZ)
    angle = 2 * np.pi / NZ * ((index[:, None] * index[None, :]) % NZ)
    return np.concatenate([np.cos(angle), np.sin(angle)], 1).astype(ml_dtypes.bfloat16)


def tap_transform():
    column = chunk_columns().reshape(-1)
    shift = np.arange(TAPS) - 3
    wave = np.exp(2j * np.pi / NX * ((column[:, None] * shift[None, :]) % NX))
    spectrum = wave @ tap_values(XBINS).T
    both = np.stack([spectrum.real, spectrum.imag])
    high = both.astype(np.float32).astype(ml_dtypes.bfloat16)
    low = (both - high.astype(np.float64)).astype(np.float32).astype(ml_dtypes.bfloat16)
    return np.concatenate([high, low], axis=2)


def sine_coefficients(terms):
    nodes = 0.25 + 0.25 * np.cos(np.pi * (np.arange(400) + 0.5) / 400)
    f = np.sqrt(nodes) * np.sqrt(0.5)
    basis = f[:, None] ** (2 * np.arange(terms)[None, :] + 1)
    scale = np.abs(basis).max(0)
    fit = np.linalg.lstsq(basis / scale, np.sin(2 * np.pi * f), rcond=None)[0]
    return [float(v) for v in fit / scale]


SINE = sine_coefficients(7)


def sine_turns(turns):
    f = turns - jnp.round(turns)
    t = f * f
    value = jnp.full_like(t, SINE[-1])
    for c in SINE[-2::-1]:
        value = value * t + c
    return value * f


def nt_dot(a, b):
    return lax.dot_general(
        a, b, (((1,), (1,)), ((), ())), preferred_element_type=jnp.float32
    )


def insertion_kernel(
    pose_ref,
    label_ref,
    focus_ref,
    images_hbm,
    xtab_hbm,
    xtap_hbm,
    ztab_hbm,
    out_ref,
    images_ref,
    xtab_ref,
    xtap_ref,
    ztab_ref,
    depth_ref,
    rows_ref,
    both_ref,
    factor_ref,
    send_ref,
    recv_ref,
    key_ref,
    keys_ref,
    spread_ref,
    zsend_ref,
    zrecv_ref,
    send_sem,
    recv_sem,
    ksend_sem,
    krecv_sem,
    zsend_sem,
    zrecv_sem,
    image_sem,
    table_sem,
    greet_sem,
):
    slab = lax.axis_index("slab")
    me_y = lax.axis_index("img")
    me_z = slab // Q
    me_q = lax.rem(slab, Q)
    me_x, me_core = me_q // 2, lax.rem(me_q, 2)
    peer_q = {
        (dx, flip): lax.rem(me_x + dx, Q // 2) * 2 + lax.rem(me_core + flip, 2)
        for dx, flip in ACROSS
    }
    peer_y = [lax.rem(me_y + dy, NY) for dy in range(NY)]
    partners = [
        (dy, across)
        for group in ROW_GROUPS
        for across in ACROSS
        for dy in group
        if (dy, across) != (0, (0, 0))
    ]

    def plane_peer(dy, across):
        return me_z * Q + peer_q[across], peer_y[dy]

    def slot_of(dy, across):
        return dy * Q + across[0] * 2 + across[1]

    def z_peer(dz):
        return lax.rem(me_z + dz, ZC) * Q + me_q, me_y

    per = IMG_DEV // LOADS
    loads = [
        pltpu.make_async_copy(
            images_hbm.at[pl.ds(n * per, per)],
            images_ref.at[pl.ds(n * per, per)],
            image_sem.at[n],
        )
        for n in range(LOADS)
    ]
    tables = [
        pltpu.make_async_copy(source, target, table_sem.at[n])
        for n, (source, target) in enumerate(
            [(xtap_hbm, xtap_ref), (xtab_hbm, xtab_ref), (ztab_hbm, ztab_ref)]
        )
    ]
    for copy in loads + tables:
        copy.start()

    barrier = pltpu.get_barrier_semaphore()

    for dz in (1, ZC - 1):
        pl.semaphore_signal(
            barrier, inc=1, device_id=z_peer(dz), device_id_type=MESH
        )

    def greet(n):
        for dz in (2**n, ZC - 2**n):
            pl.semaphore_signal(
                greet_sem.at[n], inc=1, device_id=z_peer(dz), device_id_type=MESH
            )

    def greeted(n):
        pl.semaphore_wait(greet_sem.at[n], 2)

    for partner in partners:
        pl.semaphore_signal(
            barrier, inc=1, device_id=plane_peer(*partner), device_id_type=MESH
        )

    key = label_ref[...] * (NZ * ZBINS * XBINS) + pose_ref[...]
    key_ref[...] = key
    depth_ref[...] = jnp.broadcast_to(
        focus_ref[...].astype(jnp.float32) * (200.0 / (NX * NX)), (IMG_DEV, IMG_DEV)
    ).T

    def unpack(i):
        value = jnp.concatenate(
            [images_ref[i, r].astype(jnp.float32) for r in range(2)], axis=0
        )
        for b in range(NX // 128):
            rows_ref[b, pl.ds(pl.multiple_of(i * 8, 8), 8), :] = value[
                :, b * 128 : (b + 1) * 128
            ]

    for n in range(LOADS):
        loads[n].wait()
        pl.loop(n * per, (n + 1) * per, unroll=8)(unpack)

    tables[0].wait()
    row = lax.broadcasted_iota(jnp.int32, (8, IMG_DEV), 0)
    xbin = jnp.broadcast_to(key & (XBINS - 1), (8, IMG_DEV))
    chosen = jnp.where(xbin == (row & (XBINS - 1)), 1.0, 0.0).astype(jnp.bfloat16)
    for part in range(2):
        factor_ref[part] = jnp.dot(
            xtap_ref[part], chosen, preferred_element_type=jnp.float32
        )
    tables[1].wait()

    lane = lax.broadcasted_iota(jnp.int32, (1, 128), 1)

    def weigh(ky):
        for b in range(NX // 128):
            signed = (
                ((lane + (b * 128 + NX // 2)) & (NX - 1)) - NX // 2
            )
            radius = (signed * signed + (ky + 1) * (ky + 1)).astype(jnp.float32)
            ctf = sine_turns(depth_ref[...] * radius + 0.1 / (2 * math.pi))
            for r in range(2):
                image = rows_ref[b, pl.ds(r * KY + ky, IMG_DEV, stride=8), :]
                both_ref[
                    ky, r * IMG_DEV : (r + 1) * IMG_DEV, b * 128 : (b + 1) * 128
                ] = (ctf * image).astype(jnp.bfloat16)

    def transform(chunk, ky):
        product = nt_dot(xtab_ref[chunk], both_ref[ky])
        for q in range(Q):
            top = q * 2 * ROWS
            cosine = product[top : top + ROWS]
            sine = product[top + ROWS : top + 2 * ROWS]
            real = cosine[:, :IMG_DEV] - sine[:, IMG_DEV:]
            imag = sine[:, :IMG_DEV] + cosine[:, IMG_DEV:]
            at = slice((chunk * Q + q) * ROWS, (chunk * Q + q + 1) * ROWS)
            tap_real, tap_imag = factor_ref[0, at], factor_ref[1, at]
            send_ref[chunk, ky * Q + q] = jnp.concatenate(
                [
                    real * tap_real - imag * tap_imag,
                    real * tap_imag + imag * tap_real,
                ],
                axis=0,
            ).astype(jnp.bfloat16)

    def send(chunk, dy, across):
        slot = slot_of(dy, across)
        block = send_ref.at[chunk, peer_y[dy] * Q + peer_q[across]]
        if slot == 0:
            pltpu.make_async_copy(
                block, recv_ref.at[chunk, 0], recv_sem.at[chunk, 0]
            ).start()
        else:
            pltpu.make_async_remote_copy(
                src_ref=block,
                dst_ref=recv_ref.at[chunk, slot],
                send_sem=send_sem.at[chunk],
                recv_sem=recv_sem.at[chunk, dy],
                device_id=plane_peer(dy, across),
                device_id_type=MESH,
            ).start()

    def send_keys():
        pltpu.make_async_copy(key_ref, keys_ref.at[0], krecv_sem).start()
        for partner in partners:
            pltpu.make_async_remote_copy(
                src_ref=key_ref,
                dst_ref=keys_ref.at[slot_of(*partner)],
                send_sem=ksend_sem,
                recv_sem=krecv_sem,
                device_id=plane_peer(*partner),
                device_id_type=MESH,
            ).start()

    for chunk in range(CHUNKS):
        for group in ROW_GROUPS:
            for dy in group:
                if chunk == 0:
                    weigh(peer_y[dy])
                transform(chunk, peer_y[dy])
            if chunk == 0 and group == ROW_GROUPS[0]:
                pl.semaphore_wait(barrier, PLANE - 1 + 2)
                greet(0)
                send_keys()
            for across in ACROSS:
                for dy in group:
                    send(chunk, dy, across)

    greeted(0)
    greet(1)

    pltpu.make_async_copy(keys_ref, keys_ref, krecv_sem).wait()
    ztaps = tap_values(ZBINS)
    sub = lax.broadcasted_iota(jnp.int32, (16, IMG_DEV), 0)

    def spread(slot):
        entry = keys_ref[slot]
        zbin = (entry >> 2) & (ZBINS - 1)
        start = (entry >> 4) & (NZ - 1)
        label = entry >> 13
        low = jnp.broadcast_to(start & 15, (16, IMG_DEV))
        offset = (sub - low) & 15
        base = jnp.broadcast_to(start >> 4, (16, IMG_DEV))
        base = (base + jnp.where(sub < low, 1, 0)) & 31
        block = base + jnp.broadcast_to(label * 32, (16, IMG_DEV))
        pattern = jnp.zeros((16, IMG_DEV), jnp.float32)
        for t in range(TAPS):
            tap = jnp.full((1, IMG_DEV), float(ztaps[0, t]), jnp.float32)
            for b in range(1, ZBINS):
                tap = jnp.where(zbin == b, float(ztaps[b, t]), tap)
            pattern = jnp.where(
                offset == t, jnp.broadcast_to(tap, (16, IMG_DEV)), pattern
            )
        lanes = pl.ds(pl.multiple_of(lax.rem(slot, Q) * IMG_DEV, IMG_DEV), IMG_DEV)
        block = block.astype(jnp.float32).astype(jnp.bfloat16)
        pattern = pattern.astype(jnp.bfloat16)
        for b in range(CLASSES * NZ // 16):
            spread_ref[slot // Q, b * 16 : (b + 1) * 16, lanes] = jnp.where(
                block == jnp.bfloat16(b), pattern, jnp.bfloat16(0)
            )

    pl.loop(0, PLANE // 2)(spread)
    greeted(1)
    greet(2)
    pl.loop(PLANE // 2, PLANE)(spread)

    def to_owners(chunk, volume):
        for c in range(CLASSES):
            planes = slice(c * NZ, (c + 1) * NZ)
            for k in range(KC):
                zsend_ref[c * K + chunk * KC + k] = jnp.concatenate(
                    [
                        volume[r * ROWS + k * J : r * ROWS + (k + 1) * J, planes]
                        for r in range(2)
                    ],
                    axis=0,
                ).astype(jnp.bfloat16)

        def to_z(dz):
            pltpu.make_async_remote_copy(
                src_ref=zsend_ref.at[lax.rem(me_z + dz, ZC)],
                dst_ref=zrecv_ref.at[dz],
                send_sem=zsend_sem,
                recv_sem=zrecv_sem,
                device_id=z_peer(dz),
                device_id_type=MESH,
            ).start()

        away = [lax.rem(chunk * KC + k + ZC - me_z, K) for k in range(KC)]
        for dz in away:
            to_z(dz + K)
        for dz in away:

            @pl.when(dz != 0)
            def _():
                to_z(dz)

            @pl.when(dz == 0)
            def _():
                pltpu.make_async_copy(
                    zsend_ref.at[me_z], zrecv_ref.at[0], zrecv_sem
                ).start()

    for together in TOGETHER:
        volume = None
        for dy in (dy for group in ROW_GROUPS for dy in group):
            for chunk in together:
                arrived = recv_ref.at[chunk, pl.ds(dy * Q, Q)]
                pltpu.make_async_copy(arrived, arrived, recv_sem.at[chunk, dy]).wait()
            part = nt_dot(
                jnp.concatenate(
                    [
                        jnp.concatenate(
                            [recv_ref[chunk, dy * Q + q] for q in range(Q)], axis=1
                        )
                        for chunk in together
                    ],
                    axis=0,
                ),
                spread_ref[dy],
            )
            volume = part if volume is None else volume + part
        if together == TOGETHER[0]:
            greeted(2)
        for n, chunk in enumerate(together):
            to_owners(chunk, volume[n * 2 * ROWS : (n + 1) * 2 * ROWS])

    tables[2].wait()
    pltpu.make_async_copy(zrecv_ref, zrecv_ref, zrecv_sem).wait()

    columns = jnp.zeros((2 * J, NZ), jnp.float32)
    for dz in range(ZC):
        columns = columns + zrecv_ref[dz].astype(jnp.float32)
    high = columns.astype(jnp.bfloat16)
    low = (columns - high.astype(jnp.float32)).astype(jnp.bfloat16)
    waves = jnp.dot(
        jnp.concatenate([high, low], axis=0),
        ztab_ref[...],
        preferred_element_type=jnp.float32,
    )
    waves = (waves[: 2 * J] + waves[2 * J :]) * (2.5 / math.sqrt(IMAGES * NX))
    out_ref[0] = waves[:J, :NZ] - waves[J:, NZ:]
    out_ref[1] = waves[:J, NZ:] + waves[J:, :NZ]

    for chunk in range(CHUNKS):
        plane_sent = send_ref.at[chunk, pl.ds(0, PLANE - 1)]
        pltpu.make_async_copy(plane_sent, plane_sent, send_sem.at[chunk]).wait()
    keys_sent = keys_ref.at[pl.ds(0, PLANE - 1)]
    pltpu.make_async_copy(keys_sent, keys_sent, ksend_sem).wait()
    z_sent = zsend_ref.at[pl.ds(0, ZC - 1)]
    pltpu.make_async_copy(z_sent, z_sent, zsend_sem).wait()


def on_device(images, pose_bins, labels, defocus):
    vmem = pl.BlockSpec(memory_space=pltpu.VMEM)
    out = pl.pallas_call(
        insertion_kernel,
        out_shape=jax.ShapeDtypeStruct((2, J, NZ), jnp.float32),
        in_specs=[vmem] * 3 + [pl.BlockSpec(memory_space=BIG)] * 4,
        out_specs=vmem,
        scratch_shapes=[
            pltpu.VMEM(images.shape, jnp.bfloat16),
            pltpu.VMEM((CHUNKS, 2 * NX // CHUNKS, NX), jnp.bfloat16),
            pltpu.VMEM((2, NX, 8), jnp.bfloat16),
            pltpu.VMEM((NZ, 2 * NZ), jnp.bfloat16),
            pltpu.VMEM((IMG_DEV, IMG_DEV), jnp.float32),
            pltpu.VMEM((NX // 128, IMG_DEV * 8, 128), jnp.float32),
            pltpu.VMEM((KY, 2 * IMG_DEV, NX), jnp.bfloat16),
            pltpu.VMEM((2, NX, IMG_DEV), jnp.float32),
            pltpu.VMEM((CHUNKS, PLANE, 2 * ROWS, IMG_DEV), jnp.bfloat16),
            pltpu.VMEM((CHUNKS, PLANE, 2 * ROWS, IMG_DEV), jnp.bfloat16),
            pltpu.VMEM((1, IMG_DEV), jnp.int32),
            pltpu.VMEM((PLANE, 1, IMG_DEV), jnp.int32),
            pltpu.VMEM((NY, CLASSES * NZ, Q * IMG_DEV), jnp.bfloat16),
            pltpu.VMEM((ZC, 2 * J, NZ), jnp.bfloat16),
            pltpu.VMEM((ZC, 2 * J, NZ), jnp.bfloat16),
            pltpu.SemaphoreType.DMA((CHUNKS,)),
            pltpu.SemaphoreType.DMA((CHUNKS, NY)),
            pltpu.SemaphoreType.DMA,
            pltpu.SemaphoreType.DMA,
            pltpu.SemaphoreType.DMA,
            pltpu.SemaphoreType.DMA,
            pltpu.SemaphoreType.DMA((LOADS,)),
            pltpu.SemaphoreType.DMA((3,)),
            pltpu.SemaphoreType.REGULAR((3,)),
        ],
        compiler_params=pltpu.CompilerParams(
            collective_id=0, has_side_effects=True, vmem_limit_bytes=55040 * 1024
        ),
    )(
        pose_bins.reshape(1, IMG_DEV),
        labels.reshape(1, IMG_DEV),
        defocus.reshape(1, IMG_DEV),
        images,
        jnp.asarray(x_table()),
        jnp.asarray(tap_transform()),
        jnp.asarray(z_table()),
    )
    return out.transpose(1, 0, 2)[None]


def solution(mesh):
    placed = (
        P(("slab", "img"), None, None, None),
        P(("slab", "img")),
        P(("slab", "img")),
        P(("slab", "img")),
    )
    return jax.shard_map(
        on_device,
        mesh=mesh,
        in_specs=placed,
        out_specs=P("img", "slab", None, None),
        check_vma=False,
    )
```

```python
import math

import jax
import jax.numpy as jnp
import ml_dtypes
import numpy as np
from jax import lax
from jax.experimental import pallas as pl
from jax.experimental.pallas import tpu as pltpu
from jax.sharding import PartitionSpec as P

NX = 512
KY = 4
NZ = 512
CLASSES = 2
ZBINS = 4
XBINS = 4
TAPS = 8
IMG_DEV = 128
IMAGES = 65536

ZC = 16
Q = 8
NY = 4
J = NX * CLASSES // (ZC * Q)
K = NX // (Q * J)
PLANE = NY * Q
LOADS = 4
CHUNKS = 4
KC = K // CHUNKS
ROWS = KC * J
TOGETHER = ((0,), (1,), (2,), (3,))
ACROSS = [(dx, flip) for dx in (2, 1, 3, 0) for flip in (0, 1)]
ROW_GROUPS = ((2,), (1, 3), (0,))

MESH = pl.DeviceIdType.MESH
BIG = pltpu.HBM


def tap_values(bins):
    fraction = (np.arange(bins) + 0.5) / bins
    distance = np.arange(TAPS)[None, :] - 3.0 - fraction[:, None]
    kernel = np.sinc(distance) * np.sinc(distance / 4.0)
    kernel = kernel / kernel.sum(axis=-1, keepdims=True)
    return kernel.astype(np.float32).astype(ml_dtypes.bfloat16).astype(np.float64)


def chunk_columns():
    n, q, k, j = np.meshgrid(
        np.arange(CHUNKS), np.arange(Q), np.arange(KC), np.arange(J), indexing="ij"
    )
    return (KC * n + k) * Q * J + q * J + j


def x_table():
    column = chunk_columns().reshape(CHUNKS, Q, 1, KC * J, 1)
    angle = 2 * np.pi / NX * ((column * np.arange(NX)) % NX)
    both = np.concatenate([np.cos(angle), np.sin(angle)], axis=2)
    return both.reshape(CHUNKS, Q * 2 * KC * J, NX).astype(ml_dtypes.bfloat16)


def z_table():
    index = np.arange(NZ)
    angle = 2 * np.pi / NZ * ((index[:, None] * index[None, :]) % NZ)
    return np.concatenate([np.cos(angle), np.sin(angle)], 1).astype(ml_dtypes.bfloat16)


def tap_transform():
    column = chunk_columns().reshape(-1)
    shift = np.arange(TAPS) - 3
    wave = np.exp(2j * np.pi / NX * ((column[:, None] * shift[None, :]) % NX))
    spectrum = wave @ tap_values(XBINS).T
    both = np.stack([spectrum.real, spectrum.imag])
    high = both.astype(np.float32).astype(ml_dtypes.bfloat16)
    low = (both - high.astype(np.float64)).astype(np.float32).astype(ml_dtypes.bfloat16)
    return np.concatenate([high, low], axis=2)


def sine_coefficients(terms):
    nodes = 0.25 + 0.25 * np.cos(np.pi * (np.arange(400) + 0.5) / 400)
    f = np.sqrt(nodes) * np.sqrt(0.5)
    basis = f[:, None] ** (2 * np.arange(terms)[None, :] + 1)
    scale = np.abs(basis).max(0)
    fit = np.linalg.lstsq(basis / scale, np.sin(2 * np.pi * f), rcond=None)[0]
    return [float(v) for v in fit / scale]


SINE = sine_coefficients(7)


def sine_turns(turns):
    f = turns - jnp.round(turns)
    t = f * f
    value = jnp.full_like(t, SINE[-1])
    for c in SINE[-2::-1]:
        value = value * t + c
    return value * f


def nt_dot(a, b):
    return lax.dot_general(
        a, b, (((1,), (1,)), ((), ())), preferred_element_type=jnp.float32
    )


def insertion_kernel(
    pose_ref,
    label_ref,
    focus_ref,
    images_hbm,
    xtab_hbm,
    xtap_hbm,
    ztab_hbm,
    out_ref,
    images_ref,
    xtab_ref,
    xtap_ref,
    ztab_ref,
    depth_ref,
    rows_ref,
    both_ref,
    factor_ref,
    send_ref,
    recv_ref,
    key_ref,
    keys_ref,
    spread_ref,
    zsend_ref,
    zrecv_ref,
    send_sem,
    recv_sem,
    ksend_sem,
    krecv_sem,
    zsend_sem,
    zrecv_sem,
    image_sem,
    table_sem,
    greet_sem,
):
    slab = lax.axis_index("slab")
    me_y = lax.axis_index("img")
    me_z = slab // Q
    me_q = lax.rem(slab, Q)
    me_x, me_core = me_q // 2, lax.rem(me_q, 2)
    peer_q = {
        (dx, flip): lax.rem(me_x + dx, Q // 2) * 2 + lax.rem(me_core + flip, 2)
        for dx, flip in ACROSS
    }
    peer_y = [lax.rem(me_y + dy, NY) for dy in range(NY)]
    partners = [
        (dy, across)
        for group in ROW_GROUPS
        for across in ACROSS
        for dy in group
        if (dy, across) != (0, (0, 0))
    ]

    def plane_peer(dy, across):
        return me_z * Q + peer_q[across], peer_y[dy]

    def slot_of(dy, across):
        return dy * Q + across[0] * 2 + across[1]

    def z_peer(dz):
        return lax.rem(me_z + dz, ZC) * Q + me_q, me_y

    per = IMG_DEV // LOADS
    loads = [
        pltpu.make_async_copy(
            images_hbm.at[pl.ds(n * per, per)],
            images_ref.at[pl.ds(n * per, per)],
            image_sem.at[n],
        )
        for n in range(LOADS)
    ]
    tables = [
        pltpu.make_async_copy(source, target, table_sem.at[n])
        for n, (source, target) in enumerate(
            [(xtap_hbm, xtap_ref), (xtab_hbm, xtab_ref), (ztab_hbm, ztab_ref)]
        )
    ]
    for copy in loads + tables:
        copy.start()

    barrier = pltpu.get_barrier_semaphore()

    for dz in (1, ZC - 1):
        pl.semaphore_signal(
            barrier, inc=1, device_id=z_peer(dz), device_id_type=MESH
        )

    def greet(n):
        for dz in (2**n, ZC - 2**n):
            pl.semaphore_signal(
                greet_sem.at[n], inc=1, device_id=z_peer(dz), device_id_type=MESH
            )

    def greeted(n):
        pl.semaphore_wait(greet_sem.at[n], 2)

    for partner in partners:
        pl.semaphore_signal(
            barrier, inc=1, device_id=plane_peer(*partner), device_id_type=MESH
        )

    key = label_ref[...] * (NZ * ZBINS * XBINS) + pose_ref[...]
    key_ref[...] = key
    depth_ref[...] = jnp.broadcast_to(
        focus_ref[...].astype(jnp.float32) * (200.0 / (NX * NX)), (IMG_DEV, IMG_DEV)
    ).T

    def unpack(i):
        value = jnp.concatenate(
            [images_ref[i, r].astype(jnp.float32) for r in range(2)], axis=0
        )
        for b in range(NX // 128):
            rows_ref[b, pl.ds(pl.multiple_of(i * 8, 8), 8), :] = value[
                :, b * 128 : (b + 1) * 128
            ]

    for n in range(LOADS):
        loads[n].wait()
        pl.loop(n * per, (n + 1) * per, unroll=8)(unpack)

    tables[0].wait()
    row = lax.broadcasted_iota(jnp.int32, (8, IMG_DEV), 0)
    xbin = jnp.broadcast_to(key & (XBINS - 1), (8, IMG_DEV))
    chosen = jnp.where(xbin == (row & (XBINS - 1)), 1.0, 0.0).astype(jnp.bfloat16)
    for part in range(2):
        factor_ref[part] = jnp.dot(
            xtap_ref[part], chosen, preferred_element_type=jnp.float32
        )
    tables[1].wait()

    lane = lax.broadcasted_iota(jnp.int32, (1, 128), 1)

    def weigh(ky):
        for b in range(NX // 128):
            signed = (
                ((lane + (b * 128 + NX // 2)) & (NX - 1)) - NX // 2
            )
            radius = (signed * signed + (ky + 1) * (ky + 1)).astype(jnp.float32)
            ctf = sine_turns(depth_ref[...] * radius + 0.1 / (2 * math.pi))
            for r in range(2):
                image = rows_ref[b, pl.ds(r * KY + ky, IMG_DEV, stride=8), :]
                both_ref[
                    ky, r * IMG_DEV : (r + 1) * IMG_DEV, b * 128 : (b + 1) * 128
                ] = (ctf * image).astype(jnp.bfloat16)

    def transform(chunk, ky):
        product = nt_dot(xtab_ref[chunk], both_ref[ky])
        for q in range(Q):
            top = q * 2 * ROWS
            cosine = product[top : top + ROWS]
            sine = product[top + ROWS : top + 2 * ROWS]
            real = cosine[:, :IMG_DEV] - sine[:, IMG_DEV:]
            imag = sine[:, :IMG_DEV] + cosine[:, IMG_DEV:]
            at = slice((chunk * Q + q) * ROWS, (chunk * Q + q + 1) * ROWS)
            tap_real, tap_imag = factor_ref[0, at], factor_ref[1, at]
            send_ref[chunk, ky * Q + q] = jnp.concatenate(
                [
                    real * tap_real - imag * tap_imag,
                    real * tap_imag + imag * tap_real,
                ],
                axis=0,
            ).astype(jnp.bfloat16)

    def send(chunk, dy, across):
        slot = slot_of(dy, across)
        block = send_ref.at[chunk, peer_y[dy] * Q + peer_q[across]]
        if slot == 0:
            pltpu.make_async_copy(
                block, recv_ref.at[chunk, 0], recv_sem.at[chunk, 0]
            ).start()
        else:
            pltpu.make_async_remote_copy(
                src_ref=block,
                dst_ref=recv_ref.at[chunk, slot],
                send_sem=send_sem.at[chunk],
                recv_sem=recv_sem.at[chunk, dy],
                device_id=plane_peer(dy, across),
                device_id_type=MESH,
            ).start()

    def send_keys():
        pltpu.make_async_copy(key_ref, keys_ref.at[0], krecv_sem).start()
        for partner in partners:
            pltpu.make_async_remote_copy(
                src_ref=key_ref,
                dst_ref=keys_ref.at[slot_of(*partner)],
                send_sem=ksend_sem,
                recv_sem=krecv_sem,
                device_id=plane_peer(*partner),
                device_id_type=MESH,
            ).start()

    for chunk in range(CHUNKS):
        for group in ROW_GROUPS:
            for dy in group:
                if chunk == 0:
                    weigh(peer_y[dy])
                transform(chunk, peer_y[dy])
            if chunk == 0 and group == ROW_GROUPS[0]:
                pl.semaphore_wait(barrier, PLANE - 1 + 2)
                greet(0)
                send_keys()
            for across in ACROSS:
                for dy in group:
                    send(chunk, dy, across)
        if chunk == 0:
            greeted(0)
            greet(1)

    greeted(1)
    greet(2)

    pltpu.make_async_copy(keys_ref, keys_ref, krecv_sem).wait()
    ztaps = tap_values(ZBINS)
    sub = lax.broadcasted_iota(jnp.int32, (16, IMG_DEV), 0)

    def spread(slot):
        entry = keys_ref[slot]
        zbin = (entry >> 2) & (ZBINS - 1)
        start = (entry >> 4) & (NZ - 1)
        label = entry >> 13
        low = jnp.broadcast_to(start & 15, (16, IMG_DEV))
        offset = (sub - low) & 15
        base = jnp.broadcast_to(start >> 4, (16, IMG_DEV))
        base = (base + jnp.where(sub < low, 1, 0)) & 31
        block = base + jnp.broadcast_to(label * 32, (16, IMG_DEV))
        pattern = jnp.zeros((16, IMG_DEV), jnp.float32)
        for t in range(TAPS):
            tap = jnp.full((1, IMG_DEV), float(ztaps[0, t]), jnp.float32)
            for b in range(1, ZBINS):
                tap = jnp.where(zbin == b, float(ztaps[b, t]), tap)
            pattern = jnp.where(
                offset == t, jnp.broadcast_to(tap, (16, IMG_DEV)), pattern
            )
        lanes = pl.ds(pl.multiple_of(lax.rem(slot, Q) * IMG_DEV, IMG_DEV), IMG_DEV)
        block = block.astype(jnp.float32).astype(jnp.bfloat16)
        pattern = pattern.astype(jnp.bfloat16)
        for b in range(CLASSES * NZ // 16):
            spread_ref[slot // Q, b * 16 : (b + 1) * 16, lanes] = jnp.where(
                block == jnp.bfloat16(b), pattern, jnp.bfloat16(0)
            )

    pl.loop(0, PLANE)(spread)

    def to_owners(chunk, volume):
        for c in range(CLASSES):
            planes = slice(c * NZ, (c + 1) * NZ)
            for k in range(KC):
                zsend_ref[c * K + chunk * KC + k] = jnp.concatenate(
                    [
                        volume[r * ROWS + k * J : r * ROWS + (k + 1) * J, planes]
                        for r in range(2)
                    ],
                    axis=0,
                ).astype(jnp.bfloat16)

        def to_z(dz):
            pltpu.make_async_remote_copy(
                src_ref=zsend_ref.at[lax.rem(me_z + dz, ZC)],
                dst_ref=zrecv_ref.at[dz],
                send_sem=zsend_sem,
                recv_sem=zrecv_sem,
                device_id=z_peer(dz),
                device_id_type=MESH,
            ).start()

        away = [lax.rem(chunk * KC + k + ZC - me_z, K) for k in range(KC)]
        for dz in away:
            to_z(dz + K)
        for dz in away:

            @pl.when(dz != 0)
            def _():
                to_z(dz)

            @pl.when(dz == 0)
            def _():
                pltpu.make_async_copy(
                    zsend_ref.at[me_z], zrecv_ref.at[0], zrecv_sem
                ).start()

    for together in TOGETHER:
        volume = None
        for dy in (dy for group in ROW_GROUPS for dy in group):
            for chunk in together:
                arrived = recv_ref.at[chunk, pl.ds(dy * Q, Q)]
                pltpu.make_async_copy(arrived, arrived, recv_sem.at[chunk, dy]).wait()
            part = nt_dot(
                jnp.concatenate(
                    [
                        jnp.concatenate(
                            [recv_ref[chunk, dy * Q + q] for q in range(Q)], axis=1
                        )
                        for chunk in together
                    ],
                    axis=0,
                ),
                spread_ref[dy],
            )
            volume = part if volume is None else volume + part
        if together == TOGETHER[0]:
            greeted(2)
        for n, chunk in enumerate(together):
            to_owners(chunk, volume[n * 2 * ROWS : (n + 1) * 2 * ROWS])

    tables[2].wait()
    pltpu.make_async_copy(zrecv_ref, zrecv_ref, zrecv_sem).wait()

    columns = jnp.zeros((2 * J, NZ), jnp.float32)
    for dz in range(ZC):
        columns = columns + zrecv_ref[dz].astype(jnp.float32)
    high = columns.astype(jnp.bfloat16)
    low = (columns - high.astype(jnp.float32)).astype(jnp.bfloat16)
    waves = jnp.dot(
        jnp.concatenate([high, low], axis=0),
        ztab_ref[...],
        preferred_element_type=jnp.float32,
    )
    waves = (waves[: 2 * J] + waves[2 * J :]) * (2.5 / math.sqrt(IMAGES * NX))
    out_ref[0] = waves[:J, :NZ] - waves[J:, NZ:]
    out_ref[1] = waves[:J, NZ:] + waves[J:, :NZ]

    for chunk in range(CHUNKS):
        plane_sent = send_ref.at[chunk, pl.ds(0, PLANE - 1)]
        pltpu.make_async_copy(plane_sent, plane_sent, send_sem.at[chunk]).wait()
    keys_sent = keys_ref.at[pl.ds(0, PLANE - 1)]
    pltpu.make_async_copy(keys_sent, keys_sent, ksend_sem).wait()
    z_sent = zsend_ref.at[pl.ds(0, ZC - 1)]
    pltpu.make_async_copy(z_sent, z_sent, zsend_sem).wait()


def on_device(images, pose_bins, labels, defocus):
    vmem = pl.BlockSpec(memory_space=pltpu.VMEM)
    out = pl.pallas_call(
        insertion_kernel,
        out_shape=jax.ShapeDtypeStruct((2, J, NZ), jnp.float32),
        in_specs=[vmem] * 3 + [pl.BlockSpec(memory_space=BIG)] * 4,
        out_specs=vmem,
        scratch_shapes=[
            pltpu.VMEM(images.shape, jnp.bfloat16),
            pltpu.VMEM((CHUNKS, 2 * NX // CHUNKS, NX), jnp.bfloat16),
            pltpu.VMEM((2, NX, 8), jnp.bfloat16),
            pltpu.VMEM((NZ, 2 * NZ), jnp.bfloat16),
            pltpu.VMEM((IMG_DEV, IMG_DEV), jnp.float32),
            pltpu.VMEM((NX // 128, IMG_DEV * 8, 128), jnp.float32),
            pltpu.VMEM((KY, 2 * IMG_DEV, NX), jnp.bfloat16),
            pltpu.VMEM((2, NX, IMG_DEV), jnp.float32),
            pltpu.VMEM((CHUNKS, PLANE, 2 * ROWS, IMG_DEV), jnp.bfloat16),
            pltpu.VMEM((CHUNKS, PLANE, 2 * ROWS, IMG_DEV), jnp.bfloat16),
            pltpu.VMEM((1, IMG_DEV), jnp.int32),
            pltpu.VMEM((PLANE, 1, IMG_DEV), jnp.int32),
            pltpu.VMEM((NY, CLASSES * NZ, Q * IMG_DEV), jnp.bfloat16),
            pltpu.VMEM((ZC, 2 * J, NZ), jnp.bfloat16),
            pltpu.VMEM((ZC, 2 * J, NZ), jnp.bfloat16),
            pltpu.SemaphoreType.DMA((CHUNKS,)),
            pltpu.SemaphoreType.DMA((CHUNKS, NY)),
            pltpu.SemaphoreType.DMA,
            pltpu.SemaphoreType.DMA,
            pltpu.SemaphoreType.DMA,
            pltpu.SemaphoreType.DMA,
            pltpu.SemaphoreType.DMA((LOADS,)),
            pltpu.SemaphoreType.DMA((3,)),
            pltpu.SemaphoreType.REGULAR((3,)),
        ],
        compiler_params=pltpu.CompilerParams(
            collective_id=0, has_side_effects=True, vmem_limit_bytes=55040 * 1024
        ),
    )(
        pose_bins.reshape(1, IMG_DEV),
        labels.reshape(1, IMG_DEV),
        defocus.reshape(1, IMG_DEV),
        images,
        jnp.asarray(x_table()),
        jnp.asarray(tap_transform()),
        jnp.asarray(z_table()),
    )
    return out.transpose(1, 0, 2)[None]


def solution(mesh):
    placed = (
        P(("slab", "img"), None, None, None),
        P(("slab", "img")),
        P(("slab", "img")),
        P(("slab", "img")),
    )
    return jax.shard_map(
        on_device,
        mesh=mesh,
        in_specs=placed,
        out_specs=P("img", "slab", None, None),
        check_vma=False,
    )
```

```python
import math

import jax
import jax.numpy as jnp
import ml_dtypes
import numpy as np
from jax import lax
from jax.experimental import pallas as pl
from jax.experimental.pallas import tpu as pltpu
from jax.sharding import PartitionSpec as P

NX = 512
KY = 4
NZ = 512
CLASSES = 2
ZBINS = 4
XBINS = 4
TAPS = 8
IMG_DEV = 128
IMAGES = 65536

ZC = 16
Q = 8
NY = 4
J = NX * CLASSES // (ZC * Q)
K = NX // (Q * J)
PLANE = NY * Q
LOADS = 4
CHUNKS = 4
KC = K // CHUNKS
ROWS = KC * J
TOGETHER = ((0,), (1,), (2,), (3,))
ACROSS = [(dx, flip) for dx in (2, 1, 3, 0) for flip in (0, 1)]
ROW_GROUPS = ((2,), (1, 3), (0,))

MESH = pl.DeviceIdType.MESH
BIG = pltpu.HBM


def tap_values(bins):
    fraction = (np.arange(bins) + 0.5) / bins
    distance = np.arange(TAPS)[None, :] - 3.0 - fraction[:, None]
    kernel = np.sinc(distance) * np.sinc(distance / 4.0)
    kernel = kernel / kernel.sum(axis=-1, keepdims=True)
    return kernel.astype(np.float32).astype(ml_dtypes.bfloat16).astype(np.float64)


def chunk_columns():
    n, q, k, j = np.meshgrid(
        np.arange(CHUNKS), np.arange(Q), np.arange(KC), np.arange(J), indexing="ij"
    )
    return (KC * n + k) * Q * J + q * J + j


def x_table():
    column = chunk_columns().reshape(CHUNKS, Q, 1, KC * J, 1)
    angle = 2 * np.pi / NX * ((column * np.arange(NX)) % NX)
    both = np.concatenate([np.cos(angle), np.sin(angle)], axis=2)
    return both.reshape(CHUNKS, Q * 2 * KC * J, NX).astype(ml_dtypes.bfloat16)


def z_table():
    index = np.arange(NZ)
    angle = 2 * np.pi / NZ * ((index[:, None] * index[None, :]) % NZ)
    return np.concatenate([np.cos(angle), np.sin(angle)], 1).astype(ml_dtypes.bfloat16)


def tap_transform():
    column = chunk_columns().reshape(-1)
    shift = np.arange(TAPS) - 3
    wave = np.exp(2j * np.pi / NX * ((column[:, None] * shift[None, :]) % NX))
    spectrum = wave @ tap_values(XBINS).T
    both = np.stack([spectrum.real, spectrum.imag])
    high = both.astype(np.float32).astype(ml_dtypes.bfloat16)
    low = (both - high.astype(np.float64)).astype(np.float32).astype(ml_dtypes.bfloat16)
    return np.concatenate([high, low], axis=2)


def sine_coefficients(terms):
    nodes = 0.25 + 0.25 * np.cos(np.pi * (np.arange(400) + 0.5) / 400)
    f = np.sqrt(nodes) * np.sqrt(0.5)
    basis = f[:, None] ** (2 * np.arange(terms)[None, :] + 1)
    scale = np.abs(basis).max(0)
    fit = np.linalg.lstsq(basis / scale, np.sin(2 * np.pi * f), rcond=None)[0]
    return [float(v) for v in fit / scale]


SINE = sine_coefficients(7)


def sine_turns(turns):
    f = turns - jnp.round(turns)
    t = f * f
    value = jnp.full_like(t, SINE[-1])
    for c in SINE[-2::-1]:
        value = value * t + c
    return value * f


def nt_dot(a, b):
    return lax.dot_general(
        a, b, (((1,), (1,)), ((), ())), preferred_element_type=jnp.float32
    )


def insertion_kernel(
    pose_ref,
    label_ref,
    focus_ref,
    images_hbm,
    xtab_hbm,
    xtap_hbm,
    ztab_hbm,
    out_ref,
    images_ref,
    xtab_ref,
    xtap_ref,
    ztab_ref,
    depth_ref,
    rows_ref,
    both_ref,
    factor_ref,
    send_ref,
    recv_ref,
    key_ref,
    keys_ref,
    spread_ref,
    zsend_ref,
    zrecv_ref,
    send_sem,
    recv_sem,
    ksend_sem,
    krecv_sem,
    zsend_sem,
    zrecv_sem,
    image_sem,
    table_sem,
    greet_sem,
):
    slab = lax.axis_index("slab")
    me_y = lax.axis_index("img")
    me_z = slab // Q
    me_q = lax.rem(slab, Q)
    me_x, me_core = me_q // 2, lax.rem(me_q, 2)
    peer_q = {
        (dx, flip): lax.rem(me_x + dx, Q // 2) * 2 + lax.rem(me_core + flip, 2)
        for dx, flip in ACROSS
    }
    peer_y = [lax.rem(me_y + dy, NY) for dy in range(NY)]
    partners = [
        (dy, across)
        for group in ROW_GROUPS
        for across in ACROSS
        for dy in group
        if (dy, across) != (0, (0, 0))
    ]

    def plane_peer(dy, across):
        return me_z * Q + peer_q[across], peer_y[dy]

    def slot_of(dy, across):
        return dy * Q + across[0] * 2 + across[1]

    def z_peer(dz):
        return lax.rem(me_z + dz, ZC) * Q + me_q, me_y

    per = IMG_DEV // LOADS
    loads = [
        pltpu.make_async_copy(
            images_hbm.at[pl.ds(n * per, per)],
            images_ref.at[pl.ds(n * per, per)],
            image_sem.at[n],
        )
        for n in range(LOADS)
    ]
    tables = [
        pltpu.make_async_copy(source, target, table_sem.at[n])
        for n, (source, target) in enumerate(
            [(xtap_hbm, xtap_ref), (xtab_hbm, xtab_ref), (ztab_hbm, ztab_ref)]
        )
    ]
    for copy in loads + tables:
        copy.start()

    barrier = pltpu.get_barrier_semaphore()

    for dz in (1, ZC - 1):
        pl.semaphore_signal(
            barrier, inc=1, device_id=z_peer(dz), device_id_type=MESH
        )

    def greet(n):
        for dz in (2**n, ZC - 2**n):
            pl.semaphore_signal(
                greet_sem.at[n], inc=1, device_id=z_peer(dz), device_id_type=MESH
            )

    def greeted(n):
        pl.semaphore_wait(greet_sem.at[n], 2)

    for partner in partners:
        pl.semaphore_signal(
            barrier, inc=1, device_id=plane_peer(*partner), device_id_type=MESH
        )

    key = label_ref[...] * (NZ * ZBINS * XBINS) + pose_ref[...]
    key_ref[...] = key
    depth_ref[...] = jnp.broadcast_to(
        focus_ref[...].astype(jnp.float32) * (200.0 / (NX * NX)), (IMG_DEV, IMG_DEV)
    ).T

    def unpack(i):
        value = jnp.concatenate(
            [images_ref[i, r].astype(jnp.float32) for r in range(2)], axis=0
        )
        for b in range(NX // 128):
            rows_ref[b, pl.ds(pl.multiple_of(i * 8, 8), 8), :] = value[
                :, b * 128 : (b + 1) * 128
            ]

    for n in range(LOADS):
        loads[n].wait()
        pl.loop(n * per, (n + 1) * per, unroll=8)(unpack)

    tables[0].wait()
    row = lax.broadcasted_iota(jnp.int32, (8, IMG_DEV), 0)
    xbin = jnp.broadcast_to(key & (XBINS - 1), (8, IMG_DEV))
    chosen = jnp.where(xbin == (row & (XBINS - 1)), 1.0, 0.0).astype(jnp.bfloat16)
    for part in range(2):
        factor_ref[part] = jnp.dot(
            xtap_ref[part], chosen, preferred_element_type=jnp.float32
        )
    tables[1].wait()

    lane = lax.broadcasted_iota(jnp.int32, (1, 128), 1)

    def weigh(ky):
        for b in range(NX // 128):
            signed = (
                ((lane + (b * 128 + NX // 2)) & (NX - 1)) - NX // 2
            )
            radius = (signed * signed + (ky + 1) * (ky + 1)).astype(jnp.float32)
            ctf = sine_turns(depth_ref[...] * radius + 0.1 / (2 * math.pi))
            for r in range(2):
                image = rows_ref[b, pl.ds(r * KY + ky, IMG_DEV, stride=8), :]
                both_ref[
                    ky, r * IMG_DEV : (r + 1) * IMG_DEV, b * 128 : (b + 1) * 128
                ] = (ctf * image).astype(jnp.bfloat16)

    def transform(chunk, ky):
        product = nt_dot(xtab_ref[chunk], both_ref[ky])
        for q in range(Q):
            top = q * 2 * ROWS
            cosine = product[top : top + ROWS]
            sine = product[top + ROWS : top + 2 * ROWS]
            real = cosine[:, :IMG_DEV] - sine[:, IMG_DEV:]
            imag = sine[:, :IMG_DEV] + cosine[:, IMG_DEV:]
            at = slice((chunk * Q + q) * ROWS, (chunk * Q + q + 1) * ROWS)
            tap_real, tap_imag = factor_ref[0, at], factor_ref[1, at]
            send_ref[chunk, ky * Q + q] = jnp.concatenate(
                [
                    real * tap_real - imag * tap_imag,
                    real * tap_imag + imag * tap_real,
                ],
                axis=0,
            ).astype(jnp.bfloat16)

    def send(chunk, dy, across):
        slot = slot_of(dy, across)
        block = send_ref.at[chunk, peer_y[dy] * Q + peer_q[across]]
        if slot == 0:
            pltpu.make_async_copy(
                block, recv_ref.at[chunk, 0], recv_sem.at[chunk, 0]
            ).start()
        else:
            pltpu.make_async_remote_copy(
                src_ref=block,
                dst_ref=recv_ref.at[chunk, slot],
                send_sem=send_sem.at[chunk],
                recv_sem=recv_sem.at[chunk, dy],
                device_id=plane_peer(dy, across),
                device_id_type=MESH,
            ).start()

    def send_keys():
        pltpu.make_async_copy(key_ref, keys_ref.at[0], krecv_sem).start()
        for partner in partners:
            pltpu.make_async_remote_copy(
                src_ref=key_ref,
                dst_ref=keys_ref.at[slot_of(*partner)],
                send_sem=ksend_sem,
                recv_sem=krecv_sem,
                device_id=plane_peer(*partner),
                device_id_type=MESH,
            ).start()

    for chunk in range(CHUNKS):
        for group in ROW_GROUPS:
            for dy in group:
                if chunk == 0:
                    weigh(peer_y[dy])
                transform(chunk, peer_y[dy])
            if chunk == 0 and group == ROW_GROUPS[0]:
                pl.semaphore_wait(barrier, PLANE - 1 + 2)
                greet(0)
                send_keys()
            for across in ACROSS:
                for dy in group:
                    send(chunk, dy, across)
        if chunk == 0:
            greeted(0)
            greet(1)
        if chunk == 1:
            greeted(1)
            greet(2)

    pltpu.make_async_copy(keys_ref, keys_ref, krecv_sem).wait()
    ztaps = tap_values(ZBINS)
    sub = lax.broadcasted_iota(jnp.int32, (16, IMG_DEV), 0)

    def spread(slot):
        entry = keys_ref[slot]
        zbin = (entry >> 2) & (ZBINS - 1)
        start = (entry >> 4) & (NZ - 1)
        label = entry >> 13
        low = jnp.broadcast_to(start & 15, (16, IMG_DEV))
        offset = (sub - low) & 15
        base = jnp.broadcast_to(start >> 4, (16, IMG_DEV))
        base = (base + jnp.where(sub < low, 1, 0)) & 31
        block = base + jnp.broadcast_to(label * 32, (16, IMG_DEV))
        pattern = jnp.zeros((16, IMG_DEV), jnp.float32)
        for t in range(TAPS):
            tap = jnp.full((1, IMG_DEV), float(ztaps[0, t]), jnp.float32)
            for b in range(1, ZBINS):
                tap = jnp.where(zbin == b, float(ztaps[b, t]), tap)
            pattern = jnp.where(
                offset == t, jnp.broadcast_to(tap, (16, IMG_DEV)), pattern
            )
        lanes = pl.ds(pl.multiple_of(lax.rem(slot, Q) * IMG_DEV, IMG_DEV), IMG_DEV)
        block = block.astype(jnp.float32).astype(jnp.bfloat16)
        pattern = pattern.astype(jnp.bfloat16)
        for b in range(CLASSES * NZ // 16):
            spread_ref[slot // Q, b * 16 : (b + 1) * 16, lanes] = jnp.where(
                block == jnp.bfloat16(b), pattern, jnp.bfloat16(0)
            )

    pl.loop(0, PLANE)(spread)

    def to_owners(chunk, volume):
        for c in range(CLASSES):
            planes = slice(c * NZ, (c + 1) * NZ)
            for k in range(KC):
                zsend_ref[c * K + chunk * KC + k] = jnp.concatenate(
                    [
                        volume[r * ROWS + k * J : r * ROWS + (k + 1) * J, planes]
                        for r in range(2)
                    ],
                    axis=0,
                ).astype(jnp.bfloat16)

        def to_z(dz):
            pltpu.make_async_remote_copy(
                src_ref=zsend_ref.at[lax.rem(me_z + dz, ZC)],
                dst_ref=zrecv_ref.at[dz],
                send_sem=zsend_sem,
                recv_sem=zrecv_sem,
                device_id=z_peer(dz),
                device_id_type=MESH,
            ).start()

        away = [lax.rem(chunk * KC + k + ZC - me_z, K) for k in range(KC)]
        for dz in away:
            to_z(dz + K)
        for dz in away:

            @pl.when(dz != 0)
            def _():
                to_z(dz)

            @pl.when(dz == 0)
            def _():
                pltpu.make_async_copy(
                    zsend_ref.at[me_z], zrecv_ref.at[0], zrecv_sem
                ).start()

    for together in TOGETHER:
        volume = None
        for dy in (dy for group in ROW_GROUPS for dy in group):
            for chunk in together:
                arrived = recv_ref.at[chunk, pl.ds(dy * Q, Q)]
                pltpu.make_async_copy(arrived, arrived, recv_sem.at[chunk, dy]).wait()
            part = nt_dot(
                jnp.concatenate(
                    [
                        jnp.concatenate(
                            [recv_ref[chunk, dy * Q + q] for q in range(Q)], axis=1
                        )
                        for chunk in together
                    ],
                    axis=0,
                ),
                spread_ref[dy],
            )
            volume = part if volume is None else volume + part
        if together == TOGETHER[0]:
            greeted(2)
        for n, chunk in enumerate(together):
            to_owners(chunk, volume[n * 2 * ROWS : (n + 1) * 2 * ROWS])

    tables[2].wait()
    pltpu.make_async_copy(zrecv_ref, zrecv_ref, zrecv_sem).wait()

    columns = jnp.zeros((2 * J, NZ), jnp.float32)
    for dz in range(ZC):
        columns = columns + zrecv_ref[dz].astype(jnp.float32)
    high = columns.astype(jnp.bfloat16)
    low = (columns - high.astype(jnp.float32)).astype(jnp.bfloat16)
    waves = jnp.dot(
        jnp.concatenate([high, low], axis=0),
        ztab_ref[...],
        preferred_element_type=jnp.float32,
    )
    waves = (waves[: 2 * J] + waves[2 * J :]) * (2.5 / math.sqrt(IMAGES * NX))
    out_ref[0] = waves[:J, :NZ] - waves[J:, NZ:]
    out_ref[1] = waves[:J, NZ:] + waves[J:, :NZ]

    for chunk in range(CHUNKS):
        plane_sent = send_ref.at[chunk, pl.ds(0, PLANE - 1)]
        pltpu.make_async_copy(plane_sent, plane_sent, send_sem.at[chunk]).wait()
    keys_sent = keys_ref.at[pl.ds(0, PLANE - 1)]
    pltpu.make_async_copy(keys_sent, keys_sent, ksend_sem).wait()
    z_sent = zsend_ref.at[pl.ds(0, ZC - 1)]
    pltpu.make_async_copy(z_sent, z_sent, zsend_sem).wait()


def on_device(images, pose_bins, labels, defocus):
    vmem = pl.BlockSpec(memory_space=pltpu.VMEM)
    out = pl.pallas_call(
        insertion_kernel,
        out_shape=jax.ShapeDtypeStruct((2, J, NZ), jnp.float32),
        in_specs=[vmem] * 3 + [pl.BlockSpec(memory_space=BIG)] * 4,
        out_specs=vmem,
        scratch_shapes=[
            pltpu.VMEM(images.shape, jnp.bfloat16),
            pltpu.VMEM((CHUNKS, 2 * NX // CHUNKS, NX), jnp.bfloat16),
            pltpu.VMEM((2, NX, 8), jnp.bfloat16),
            pltpu.VMEM((NZ, 2 * NZ), jnp.bfloat16),
            pltpu.VMEM((IMG_DEV, IMG_DEV), jnp.float32),
            pltpu.VMEM((NX // 128, IMG_DEV * 8, 128), jnp.float32),
            pltpu.VMEM((KY, 2 * IMG_DEV, NX), jnp.bfloat16),
            pltpu.VMEM((2, NX, IMG_DEV), jnp.float32),
            pltpu.VMEM((CHUNKS, PLANE, 2 * ROWS, IMG_DEV), jnp.bfloat16),
            pltpu.VMEM((CHUNKS, PLANE, 2 * ROWS, IMG_DEV), jnp.bfloat16),
            pltpu.VMEM((1, IMG_DEV), jnp.int32),
            pltpu.VMEM((PLANE, 1, IMG_DEV), jnp.int32),
            pltpu.VMEM((NY, CLASSES * NZ, Q * IMG_DEV), jnp.bfloat16),
            pltpu.VMEM((ZC, 2 * J, NZ), jnp.bfloat16),
            pltpu.VMEM((ZC, 2 * J, NZ), jnp.bfloat16),
            pltpu.SemaphoreType.DMA((CHUNKS,)),
            pltpu.SemaphoreType.DMA((CHUNKS, NY)),
            pltpu.SemaphoreType.DMA,
            pltpu.SemaphoreType.DMA,
            pltpu.SemaphoreType.DMA,
            pltpu.SemaphoreType.DMA,
            pltpu.SemaphoreType.DMA((LOADS,)),
            pltpu.SemaphoreType.DMA((3,)),
            pltpu.SemaphoreType.REGULAR((3,)),
        ],
        compiler_params=pltpu.CompilerParams(
            collective_id=0, has_side_effects=True, vmem_limit_bytes=55040 * 1024
        ),
    )(
        pose_bins.reshape(1, IMG_DEV),
        labels.reshape(1, IMG_DEV),
        defocus.reshape(1, IMG_DEV),
        images,
        jnp.asarray(x_table()),
        jnp.asarray(tap_transform()),
        jnp.asarray(z_table()),
    )
    return out.transpose(1, 0, 2)[None]


def solution(mesh):
    placed = (
        P(("slab", "img"), None, None, None),
        P(("slab", "img")),
        P(("slab", "img")),
        P(("slab", "img")),
    )
    return jax.shard_map(
        on_device,
        mesh=mesh,
        in_specs=placed,
        out_specs=P("img", "slab", None, None),
        check_vma=False,
    )
```
